32 devices in a mesh: row: 8 (over y, x, core), col: 4 (over z).
Axes of the slice: x: 2, y: 2, z: 4, core: 2. Of those that a mesh axis runs over, the one named last changes fastest.
Arguments:
- pooled: bfloat16 [4096, 1152], P(('row', 'col')), may hold values from -6 to 6
- text_embed: bfloat16 [4096, 1152], P(('row', 'col')), may hold values from -0.29882812 to 0.29882812
- head_weight: bfloat16 [1152, 1152], replicated, may hold values from -0.1875 to 0.1875
- logit_scale: float32 [4], replicated, may hold values from 1 to 4
- logit_bias: float32 [4], replicated, may hold values from -2 to 0
- partner: int32 [32, 128], P(('row', 'col')), may hold values from 0 to 127, each once within a row
Outputs:
- text_grad: float32 [4096, 1152], P(('row', 'col'))
- head_grad: float32 [1152, 1152], P('row', 'col')
The draws below stay inside these ranges and needn't reach their ends.
Inputs may be any that keep to these rules, and one draw needn't show every extreme that they name: Each row of partner is a permutation of the indices within a block.
All inputs are finite; a program needn't handle non-finite values.
Results may differ from the reference program's by a relative error of at most 0.004.
Values may be sent and summed in bfloat16 or wider, within the bound.
A program may use at most 64 MiB of HBM per device.

```python
import math
import jax
import jax.numpy as jnp
from jax import lax

D = 1152
PAIRS_DEV = 128
BLOCKS = 32
PAIRS = 4096
N_ROW = 8
N_COL = 4


def level_of(key, shape, cuts, least, top_value):
    level, own = 1.0, jax.random.fold_in(key, 6)
    for position, shards_of in cuts:
        heights = jnp.exp(jax.random.uniform(jax.random.fold_in(own, position), (shards_of,), jnp.float32, least / len(cuts), top_value / len(cuts)))
        level = level * jnp.repeat(heights, shape[position] // shards_of).reshape([-1 if axis == position else 1 for axis in range(len(shape))])
    return level


def noise(stream_key, shape, spread, bound, pieces=(), kind=jnp.bfloat16):
    array = jax.random.normal(stream_key, shape, jnp.float32) * spread
    if len(pieces) > 0:
        array = level_of(stream_key, shape, pieces, -0.22, 0.18) * array
    return jnp.clip(array, min=-bound, max=bound).astype(kind)


def setup_inputs(seed: int = 0) -> dict:
    arg_keys = jax.random.split(jax.random.key(seed), 7)
    return {
        "pooled": noise(arg_keys[0], (PAIRS, D), 1.0, 6.0, ((0, 32),)),
        "text_embed": noise(arg_keys[1], (PAIRS, D), 0.05, 0.29882812, ((0, 32),)),
        "head_weight": noise(arg_keys[2], (D, D), D ** -0.5, 0.1875),
        "logit_scale": jnp.clip(jnp.exp(jax.random.uniform(arg_keys[3], (4,), jnp.float32, math.log(1.0), math.log(4.0))), 1.0, 4.0),
        "logit_bias": jnp.clip(jax.random.uniform(arg_keys[4], (4,), jnp.float32, -2.0, 0.0), -2.0, 0.0),
        "partner": jax.vmap(lambda own: jax.random.permutation(own, PAIRS_DEV))(jax.random.split(arg_keys[5], BLOCKS)).reshape((BLOCKS, PAIRS_DEV)).astype(jnp.int32),
    }


def segment_weights(image_part, text_part, positive, logit_scale, logit_bias, factor):
    model_width = image_part.shape[1]
    bounds = [0, model_width // 8, model_width // 4, model_width // 2, model_width]
    running = jnp.zeros((image_part.shape[0], text_part.shape[0]), jnp.float32)
    level_grads = []
    for prefix in range(4):
        low_end = bounds[prefix]
        high_end = bounds[prefix + 1]
        running = running + jnp.dot(image_part[:, low_end:high_end], text_part[:, low_end:high_end].T, preferred_element_type=jnp.float32)
        logits = logit_scale[prefix] * running + logit_bias[prefix]
        level_grads.append((jax.nn.sigmoid(logits) - positive) * factor)
    weights = []
    carried = jnp.zeros_like(running)
    for prefix in range(3, -1, -1):
        carried = carried + logit_scale[prefix] * level_grads[prefix]
        weights.insert(0, carried.astype(jnp.bfloat16))
    return (weights, bounds)

def apply_weights(weights, bounds, image_part, text_part):
    image_pieces = []
    text_pieces = []
    for prefix in range(4):
        low_end = bounds[prefix]
        high_end = bounds[prefix + 1]
        image_pieces.append(jnp.dot(weights[prefix], text_part[:, low_end:high_end], preferred_element_type=jnp.float32))
        text_pieces.append(jnp.dot(weights[prefix].T, image_part[:, low_end:high_end], preferred_element_type=jnp.float32))
    return (jnp.concatenate(image_pieces, 1), jnp.concatenate(text_pieces, 1))

def reference(pooled, text_embed, head_weight, logit_scale, logit_bias, partner):
    pair_count = pooled.shape[0]
    model_width = pooled.shape[1]
    block_rows = partner.shape[1]
    factor = 1.0 / math.sqrt(pair_count)
    embedding = jnp.dot(pooled, head_weight, preferred_element_type=jnp.float32).astype(jnp.bfloat16)
    shape_four = (N_ROW, N_COL, block_rows, model_width)
    emb_blocks = embedding.reshape(shape_four)
    emb_ahead = jnp.roll(emb_blocks, -1, axis=0)
    pooled_blocks = pooled.reshape(shape_four)
    pooled_ahead = jnp.roll(pooled_blocks, -1, axis=0)
    text_blocks = text_embed.reshape(shape_four)
    partner_blocks = partner.reshape(N_ROW, N_COL, block_rows)
    local_ids = jnp.arange(block_rows, dtype=jnp.int32)

    def one_block(emb_own, emb_next, text_own, partner_own):
        positive = (partner_own[:, None] == local_ids[None, :]).astype(jnp.float32)
        weights, bounds = segment_weights(emb_own, text_own, positive, logit_scale, logit_bias, factor)
        own_image, own_text = apply_weights(weights, bounds, emb_own, text_own)
        empty = jnp.zeros((block_rows, block_rows), jnp.float32)
        weights, bounds = segment_weights(emb_next, text_own, empty, logit_scale, logit_bias, factor)
        next_image, next_text = apply_weights(weights, bounds, emb_next, text_own)
        return (own_image, next_image, own_text + next_text)

    def advance(carry, inputs):
        emb_own, emb_next, text_own, partner_own, pool_own, pool_next = inputs
        own_image, next_image, text_terms = jax.vmap(one_block)(emb_own, emb_next, text_own, partner_own)
        flat_own = pool_own.reshape(-1, model_width).astype(jnp.float32)
        flat_next = pool_next.reshape(-1, model_width).astype(jnp.float32)
        carry = carry + jnp.dot(flat_own.T, own_image.reshape(-1, model_width), precision=lax.Precision.HIGHEST)
        carry = carry + jnp.dot(flat_next.T, next_image.reshape(-1, model_width), precision=lax.Precision.HIGHEST)
        return (carry, text_terms)
    start_grad = jnp.zeros((model_width, model_width), jnp.float32)
    head_grad, text_terms = lax.scan(advance, start_grad, (emb_blocks, emb_ahead, text_blocks, partner_blocks, pooled_blocks, pooled_ahead))
    text_grad = text_terms.reshape(pair_count, model_width)
    return (text_grad, head_grad)
```

```python
import functools
import math

import jax
import jax.numpy as jnp
from jax import lax
from jax.experimental import pallas as pl
from jax.experimental.pallas import tpu as pltpu
from jax.sharding import PartitionSpec as P

LANES = 128
MESH = pl.DeviceIdType.MESH


def shifted(value, axis, by):
    count = lax.axis_size(axis)
    return lax.ppermute(value, axis, [(i, (i + by) % count) for i in range(count)])


def segment_weights(image_part, text_part, positive, logit_scale, logit_bias, factor):
    model_width = image_part.shape[1]
    bounds = [0, model_width // 8, model_width // 4, model_width // 2, model_width]
    running = jnp.zeros((image_part.shape[0], text_part.shape[0]), jnp.float32)
    level_grads = []
    for prefix in range(4):
        low_end = bounds[prefix]
        high_end = bounds[prefix + 1]
        running = running + jnp.dot(
            image_part[:, low_end:high_end],
            text_part[:, low_end:high_end].T,
            preferred_element_type=jnp.float32,
        )
        logits = logit_scale[prefix] * running + logit_bias[prefix]
        level_grads.append((jax.nn.sigmoid(logits) - positive) * factor)
    weights = []
    carried = jnp.zeros_like(running)
    for prefix in range(3, -1, -1):
        carried = carried + logit_scale[prefix] * level_grads[prefix]
        weights.insert(0, carried.astype(jnp.bfloat16))
    return (weights, bounds)


def image_side(weights, bounds, text_part):
    pieces = []
    for prefix in range(4):
        pieces.append(
            jnp.dot(
                weights[prefix],
                text_part[:, bounds[prefix] : bounds[prefix + 1]],
                preferred_element_type=jnp.float32,
            )
        )
    return jnp.concatenate(pieces, 1)


def text_side(weights, bounds, image_part):
    pieces = []
    for prefix in range(4):
        pieces.append(
            jnp.dot(
                weights[prefix].T,
                image_part[:, bounds[prefix] : bounds[prefix + 1]],
                preferred_element_type=jnp.float32,
            )
        )
    return jnp.concatenate(pieces, 1)


def body(pooled, text_embed, head_weight, logit_scale, logit_bias, partner):
    block_rows = pooled.shape[0]
    factor = 1.0 / math.sqrt(block_rows * lax.axis_size("row") * lax.axis_size("col"))
    embedding = jnp.dot(pooled, head_weight, preferred_element_type=jnp.float32).astype(
        jnp.bfloat16
    )
    local_ids = jnp.arange(block_rows, dtype=jnp.int32)
    positive = (partner[0][:, None] == local_ids[None, :]).astype(jnp.float32)
    empty = jnp.zeros((block_rows, block_rows), jnp.float32)
    weights, bounds = segment_weights(
        embedding, text_embed, positive, logit_scale, logit_bias, factor
    )
    own_image = image_side(weights, bounds, text_embed)
    own_text = text_side(weights, bounds, embedding)
    behind = shifted(text_embed, "row", 1)
    weights, bounds = segment_weights(embedding, behind, empty, logit_scale, logit_bias, factor)
    cross_image = image_side(weights, bounds, behind)
    cross_text = text_side(weights, bounds, embedding)
    returned = shifted(cross_text.astype(jnp.bfloat16), "row", -1).astype(cross_text.dtype)
    text_grad = own_text + returned
    image_grad = own_image + cross_image
    column_block = lax.all_to_all(
        image_grad.astype(jnp.bfloat16), "col", split_axis=1, concat_axis=0, tiled=True
    ).astype(image_grad.dtype)
    group_rows = lax.all_gather(pooled, "col", axis=0, tiled=True)
    block_term = jnp.dot(
        group_rows.astype(jnp.float32).T, column_block, precision=lax.Precision.HIGHEST
    )
    head_grad = lax.psum_scatter(block_term, "row", scatter_dimension=0, tiled=True)
    return (text_grad, head_grad)


def dot_nt(left, right):
    return lax.dot_general(
        left, right, (((1,), (1,)), ((), ())), preferred_element_type=jnp.float32
    )


def dot_nn(left, right):
    return jnp.dot(left, right, preferred_element_type=jnp.float32)


def aligned(low_end, high_end):
    return low_end // LANES * LANES, -(-high_end // LANES) * LANES


def weights_of(score_of, positive, scale_ref, bias_ref, factor):
    running = None
    level_grads = []
    for prefix in range(4):
        part = score_of(prefix)
        running = part if running is None else running + part
        gate = jax.nn.sigmoid(scale_ref[prefix] * running + bias_ref[prefix])
        if positive is not None:
            gate = gate - positive
        level_grads.append(gate * factor)
    weights = [None] * 4
    carried = None
    for prefix in range(3, -1, -1):
        term = scale_ref[prefix] * level_grads[prefix]
        carried = term if carried is None else carried + term
        weights[prefix] = carried.astype(jnp.bfloat16)
    return weights


def by_tile(piece_of, bounds, store):
    pieces = []
    for q in range(4):
        start, stop = aligned(bounds[q], bounds[q + 1])
        pieces.append((start, stop, piece_of(q, start, stop)))
    for tile in range(bounds[4] // LANES):
        base = tile * LANES
        value = None
        for q in range(4):
            start, stop, piece = pieces[q]
            if start <= base < stop:
                here = piece[:, base - start : base - start + LANES]
                if value is None:
                    value = here
                else:
                    lane = lax.broadcasted_iota(jnp.int32, here.shape, 1)
                    value = jnp.where(lane < bounds[q] - base, value, here)
        store(base, value)


def kernel(
    n_row,
    n_col,
    factor,
    pooled_ref,
    text_ref,
    weight_ref,
    scale_ref,
    bias_ref,
    partner_ref,
    text_grad_ref,
    head_grad_ref,
    pooled_ahead,
    text_behind,
    pooled_t,
    pooled_cols,
    embed,
    masked,
    image,
    total,
    sent,
    landed,
    near_send,
    near_recv,
    pool_send,
    pool_recv,
    image_send,
    image_recv,
    out_send,
    out_recv,
):
    rows, width = pooled_ref.shape
    chips = n_row // 2
    head_rows = width // n_row
    head_cols = width // n_col
    window = landed.shape[2]
    bounds = [0, width // 8, width // 4, width // 2, width]
    row = lax.axis_index("row")
    col = lax.axis_index("col")
    chip = row // 2
    core = row % 2

    def peer(k, e):
        other = core if e == 0 else 1 - core
        return ((chip + k) % chips) * 2 + other

    barrier = pltpu.get_barrier_semaphore()
    for d in range(1, n_row):
        pl.semaphore_signal(
            barrier, inc=1, device_id=((row + d) % n_row, col), device_id_type=MESH
        )
    for d in range(1, n_col):
        pl.semaphore_signal(
            barrier, inc=1, device_id=(row, (col + d) % n_col), device_id_type=MESH
        )

    def remote(src, dst, send, recv, device):
        return pltpu.make_async_remote_copy(
            src_ref=src,
            dst_ref=dst,
            send_sem=send,
            recv_sem=recv,
            device_id=device,
            device_id_type=MESH,
        )

    behind_copy = remote(
        text_ref, text_behind, near_send.at[0], near_recv.at[0], ((row + 1) % n_row, col)
    )
    ahead_copy = remote(
        pooled_ref,
        pooled_ahead,
        near_send.at[1],
        near_recv.at[1],
        ((row + n_row - 1) % n_row, col),
    )
    pl.semaphore_wait(barrier, n_row + n_col - 2)
    behind_copy.start()
    ahead_copy.start()

    for tile in range(width // LANES):
        lanes = pl.ds(tile * LANES, LANES)
        pooled_t[lanes, :] = pooled_ref[:, lanes].T
    pool_copies = []
    for k in range(chips):
        for e in range(2):
            slot = 2 * k + e
            if slot == 0:
                continue
            target = peer(k, e)
            copy = remote(
                pooled_t.at[pl.ds(pl.multiple_of(target * head_rows, 16), head_rows), :],
                pooled_cols.at[:, pl.ds(slot * rows, rows)],
                pool_send.at[slot],
                pool_recv.at[slot],
                (target, col),
            )
            copy.start()
            pool_copies.append(copy)
    pooled_cols[:, pl.ds(0, rows)] = pooled_t[
        pl.ds(pl.multiple_of(row * head_rows, 16), head_rows), :
    ]

    def fill_embed(source):
        at = 0
        for q in range(4):
            start, stop = aligned(bounds[q], bounds[q + 1])
            at += stop - start
        step = 3 * LANES if width % (3 * LANES) == 0 else LANES
        for base in range(0, width, step):
            part = dot_nn(source[...], weight_ref[:, pl.ds(base, step)])
            embed[:, pl.ds(base, step)] = part.astype(jnp.bfloat16)
        at = 0
        for q in range(4):
            start, stop = aligned(bounds[q], bounds[q + 1])
            part = embed[:, pl.ds(start, stop - start)].astype(jnp.float32)
            lane = lax.broadcasted_iota(jnp.int32, part.shape, 1) + start
            keep = (lane >= bounds[q]) & (lane < bounds[q + 1])
            masked[:, pl.ds(at, stop - start)] = jnp.where(keep, part, 0.0).astype(
                jnp.bfloat16
            )
            at += stop - start

    def masked_part(q):
        at = 0
        for before in range(q):
            start, stop = aligned(bounds[before], bounds[before + 1])
            at += stop - start
        start, stop = aligned(bounds[q], bounds[q + 1])
        return masked[:, pl.ds(at, stop - start)]

    def text_part(ref, q):
        start, stop = aligned(bounds[q], bounds[q + 1])
        return ref[:, pl.ds(start, stop - start)]

    fill_embed(pooled_ref)
    text_id = lax.broadcasted_iota(jnp.int32, (rows, rows), 0)
    positive = (text_id == partner_ref[...]).astype(jnp.float32).T
    own = weights_of(
        lambda q: dot_nt(masked_part(q), text_part(text_ref, q)),
        positive,
        scale_ref,
        bias_ref,
        factor,
    )
    behind_copy.wait_recv()
    cross = weights_of(
        lambda q: dot_nt(masked_part(q), text_part(text_behind, q)),
        None,
        scale_ref,
        bias_ref,
        factor,
    )

    def image_piece(q, start, stop):
        lanes = pl.ds(start, stop - start)
        return dot_nn(own[q], text_ref[:, lanes]) + dot_nn(cross[q], text_behind[:, lanes])

    def store_image(base, value):
        image[pl.ds(0, rows), pl.ds(base, LANES)] = value.astype(jnp.bfloat16)

    by_tile(image_piece, bounds, store_image)

    def slot_rows(slot):
        return image.at[pl.ds(slot * rows, rows), :]

    image_copies = {}
    for slot in [1] + [2 * k for k in range(1, chips)]:
        image_copies[slot] = remote(
            slot_rows(0),
            slot_rows(slot),
            image_send.at[slot],
            image_recv.at[slot],
            (peer(slot // 2, slot % 2), col),
        )
        image_copies[slot].start()

    def own_text_piece(q, start, stop):
        return dot_nn(own[q].T, embed[:, pl.ds(start, stop - start)])

    def store_text(base, value):
        text_grad_ref[:, pl.ds(base, LANES)] = value

    by_tile(own_text_piece, bounds, store_text)

    ahead_copy.wait_recv()
    fill_embed(pooled_ahead)
    ahead = weights_of(
        lambda q: dot_nt(text_part(text_ref, q), masked_part(q)),
        None,
        scale_ref,
        bias_ref,
        factor,
    )

    def ahead_piece(q, start, stop):
        return dot_nn(ahead[q], embed[:, pl.ds(start, stop - start)])

    def add_text(base, value):
        lanes = pl.ds(base, LANES)
        text_grad_ref[:, lanes] = text_grad_ref[:, lanes] + value

    by_tile(ahead_piece, bounds, add_text)

    for k in range(1, chips):
        slot = 2 * k
        image_copies[slot].wait_recv()
        image_copies[slot + 1] = remote(
            slot_rows(slot),
            slot_rows(slot + 1),
            image_send.at[slot + 1],
            image_recv.at[slot + 1],
            (peer(0, 1), col),
        )
        image_copies[slot + 1].start()
    for copy in pool_copies:
        copy.wait_recv()
    image_copies[1].wait_recv()
    for k in range(1, chips):
        image_copies[2 * k + 1].wait_recv()
    step = 3 * LANES if width % (3 * LANES) == 0 else LANES
    for base in range(0, width, step):
        lanes = pl.ds(base, step)
        part = dot_nn(pooled_cols[...], image[:, lanes])
        total[:, lanes] = part
        sent[:, lanes] = part.astype(jnp.bfloat16)

    def out_copy(d):
        target = (col + d) % n_col
        first = pl.multiple_of(target * head_cols // LANES * LANES, LANES)
        return remote(
            sent.at[:, pl.ds(first, window)],
            landed.at[d - 1],
            out_send.at[d - 1],
            out_recv.at[d - 1],
            (row, target),
        )

    out_copies = [out_copy(d) for d in range(n_col - 1, 0, -1)]
    for copy in out_copies:
        copy.start()
    mine = col * head_cols // LANES * LANES
    result = total[:, pl.ds(pl.multiple_of(mine, LANES), window)]
    for d in range(1, n_col):
        out_copies[n_col - 1 - d].wait_recv()
        result = result + landed[d - 1].astype(jnp.float32)
    offset = col * head_cols - mine
    head_grad_ref[...] = pltpu.roll(result, (window - offset) % window, 1)[:, :head_cols]

    behind_copy.wait_send()
    ahead_copy.wait_send()
    for copy in pool_copies:
        copy.wait_send()
    for slot in sorted(image_copies):
        image_copies[slot].wait_send()
    for copy in out_copies:
        copy.wait_send()


def window_of(width, n_col):
    head_cols = width // n_col
    spans = [aligned(c * head_cols, (c + 1) * head_cols) for c in range(n_col)]
    window = max(stop - start for start, stop in spans)
    fits = all(start + window <= width for start, _ in spans)
    return window, fits


def fused_body(n_row, n_col, pooled, text_embed, head_weight, logit_scale, logit_bias, partner):
    rows, width = pooled.shape
    factor = 1.0 / math.sqrt(rows * n_row * n_col)
    window, _ = window_of(width, n_col)
    bounds = [0, width // 8, width // 4, width // 2, width]
    spans = [aligned(bounds[q], bounds[q + 1]) for q in range(4)]
    masked_width = sum(stop - start for start, stop in spans)
    head_rows, head_cols = width // n_row, width // n_col
    vmem = pl.BlockSpec(memory_space=pltpu.VMEM)
    smem = pl.BlockSpec(memory_space=pltpu.SMEM)
    dma = pltpu.SemaphoreType.DMA
    return pl.pallas_call(
        functools.partial(kernel, n_row, n_col, factor),
        out_shape=(
            jax.ShapeDtypeStruct((rows, width), jnp.float32),
            jax.ShapeDtypeStruct((head_rows, head_cols), jnp.float32),
        ),
        in_specs=[vmem, vmem, vmem, smem, smem, vmem],
        out_specs=(vmem, vmem),
        scratch_shapes=[
            pltpu.VMEM((rows, width), jnp.bfloat16),
            pltpu.VMEM((rows, width), jnp.bfloat16),
            pltpu.VMEM((width, rows), jnp.bfloat16),
            pltpu.VMEM((head_rows, n_row * rows), jnp.bfloat16),
            pltpu.VMEM((rows, width), jnp.bfloat16),
            pltpu.VMEM((rows, masked_width), jnp.bfloat16),
            pltpu.VMEM((n_row * rows, width), jnp.bfloat16),
            pltpu.VMEM((head_rows, width), jnp.float32),
            pltpu.VMEM((head_rows, width), jnp.bfloat16),
            pltpu.VMEM((n_col - 1, head_rows, window), jnp.bfloat16),
            dma((2,)),
            dma((2,)),
            dma((n_row,)),
            dma((n_row,)),
            dma((n_row,)),
            dma((n_row,)),
            dma((n_col - 1,)),
            dma((n_col - 1,)),
        ],
        compiler_params=pltpu.CompilerParams(collective_id=0, has_side_effects=True),
    )(pooled, text_embed, head_weight, logit_scale, logit_bias, partner)


def per_device(n_row, n_col):
    def run(pooled, text_embed, head_weight, logit_scale, logit_bias, partner):
        rows, width = pooled.shape
        fused = (
            n_row % 2 == 0
            and n_col > 1
            and rows == LANES
            and width % LANES == 0
            and width % (16 * n_row) == 0
            and width % n_col == 0
            and window_of(width, n_col)[1]
        )
        args = (pooled, text_embed, head_weight, logit_scale, logit_bias, partner)
        return fused_body(n_row, n_col, *args) if fused else body(*args)

    return run


def solution(mesh):
    in_specs = (
        P(("row", "col"), None),
        P(("row", "col"), None),
        P(),
        P(),
        P(),
        P(("row", "col"), None),
    )
    out_specs = (P(("row", "col"), None), P("row", "col"))
    run = per_device(mesh.shape["row"], mesh.shape["col"])
    return jax.shard_map(run, mesh=mesh, in_specs=in_specs, out_specs=out_specs, check_vma=False)
```

```python
import functools
import math

import jax
import jax.numpy as jnp
from jax import lax
from jax.experimental import pallas as pl
from jax.experimental.pallas import tpu as pltpu
from jax.sharding import PartitionSpec as P

LANES = 128
MESH = pl.DeviceIdType.MESH


def shifted(value, axis, by):
    count = lax.axis_size(axis)
    return lax.ppermute(value, axis, [(i, (i + by) % count) for i in range(count)])


def segment_weights(image_part, text_part, positive, logit_scale, logit_bias, factor):
    model_width = image_part.shape[1]
    bounds = [0, model_width // 8, model_width // 4, model_width // 2, model_width]
    running = jnp.zeros((image_part.shape[0], text_part.shape[0]), jnp.float32)
    level_grads = []
    for prefix in range(4):
        low_end = bounds[prefix]
        high_end = bounds[prefix + 1]
        running = running + jnp.dot(
            image_part[:, low_end:high_end],
            text_part[:, low_end:high_end].T,
            preferred_element_type=jnp.float32,
        )
        logits = logit_scale[prefix] * running + logit_bias[prefix]
        level_grads.append((jax.nn.sigmoid(logits) - positive) * factor)
    weights = []
    carried = jnp.zeros_like(running)
    for prefix in range(3, -1, -1):
        carried = carried + logit_scale[prefix] * level_grads[prefix]
        weights.insert(0, carried.astype(jnp.bfloat16))
    return (weights, bounds)


def image_side(weights, bounds, text_part):
    pieces = []
    for prefix in range(4):
        pieces.append(
            jnp.dot(
                weights[prefix],
                text_part[:, bounds[prefix] : bounds[prefix + 1]],
                preferred_element_type=jnp.float32,
            )
        )
    return jnp.concatenate(pieces, 1)


def text_side(weights, bounds, image_part):
    pieces = []
    for prefix in range(4):
        pieces.append(
            jnp.dot(
                weights[prefix].T,
                image_part[:, bounds[prefix] : bounds[prefix + 1]],
                preferred_element_type=jnp.float32,
            )
        )
    return jnp.concatenate(pieces, 1)


def body(pooled, text_embed, head_weight, logit_scale, logit_bias, partner):
    block_rows = pooled.shape[0]
    factor = 1.0 / math.sqrt(block_rows * lax.axis_size("row") * lax.axis_size("col"))
    embedding = jnp.dot(pooled, head_weight, preferred_element_type=jnp.float32).astype(
        jnp.bfloat16
    )
    local_ids = jnp.arange(block_rows, dtype=jnp.int32)
    positive = (partner[0][:, None] == local_ids[None, :]).astype(jnp.float32)
    empty = jnp.zeros((block_rows, block_rows), jnp.float32)
    weights, bounds = segment_weights(
        embedding, text_embed, positive, logit_scale, logit_bias, factor
    )
    own_image = image_side(weights, bounds, text_embed)
    own_text = text_side(weights, bounds, embedding)
    behind = shifted(text_embed, "row", 1)
    weights, bounds = segment_weights(embedding, behind, empty, logit_scale, logit_bias, factor)
    cross_image = image_side(weights, bounds, behind)
    cross_text = text_side(weights, bounds, embedding)
    returned = shifted(cross_text.astype(jnp.bfloat16), "row", -1).astype(cross_text.dtype)
    text_grad = own_text + returned
    image_grad = own_image + cross_image
    column_block = lax.all_to_all(
        image_grad.astype(jnp.bfloat16), "col", split_axis=1, concat_axis=0, tiled=True
    ).astype(image_grad.dtype)
    group_rows = lax.all_gather(pooled, "col", axis=0, tiled=True)
    block_term = jnp.dot(
        group_rows.astype(jnp.float32).T, column_block, precision=lax.Precision.HIGHEST
    )
    head_grad = lax.psum_scatter(block_term, "row", scatter_dimension=0, tiled=True)
    return (text_grad, head_grad)


def dot_nt(left, right):
    return lax.dot_general(
        left, right, (((1,), (1,)), ((), ())), preferred_element_type=jnp.float32
    )


def dot_nn(left, right):
    return jnp.dot(left, right, preferred_element_type=jnp.float32)


def aligned(low_end, high_end):
    return low_end // LANES * LANES, -(-high_end // LANES) * LANES


def weights_of(score_of, positive, scale_ref, bias_ref, factor):
    running = None
    level_grads = []
    for prefix in range(4):
        part = score_of(prefix)
        running = part if running is None else running + part
        gate = jax.nn.sigmoid(scale_ref[prefix] * running + bias_ref[prefix])
        if positive is not None:
            gate = gate - positive
        level_grads.append(gate * factor)
    weights = [None] * 4
    carried = None
    for prefix in range(3, -1, -1):
        term = scale_ref[prefix] * level_grads[prefix]
        carried = term if carried is None else carried + term
        weights[prefix] = carried.astype(jnp.bfloat16)
    return weights


def by_tile(piece_of, bounds, store):
    pieces = []
    for q in range(4):
        start, stop = aligned(bounds[q], bounds[q + 1])
        pieces.append((start, stop, piece_of(q, start, stop)))
    for tile in range(bounds[4] // LANES):
        base = tile * LANES
        value = None
        for q in range(4):
            start, stop, piece = pieces[q]
            if start <= base < stop:
                here = piece[:, base - start : base - start + LANES]
                if value is None:
                    value = here
                else:
                    lane = lax.broadcasted_iota(jnp.int32, here.shape, 1)
                    value = jnp.where(lane < bounds[q] - base, value, here)
        store(base, value)


def kernel(
    n_row,
    n_col,
    factor,
    chunks,
    ready,
    window,
    tail_rows,
    pooled_ref,
    text_ref,
    weight_ref,
    scale_ref,
    bias_ref,
    partner_ref,
    text_grad_ref,
    head_grad_ref,
    pooled_ahead,
    text_behind,
    pooled_t,
    pooled_cols,
    embed,
    masked,
    image,
    total,
    sent,
    landed,
    near_send,
    near_recv,
    pool_send,
    pool_recv,
    image_send,
    image_recv,
    out_send,
    out_recv,
):
    rows, width = pooled_ref.shape
    chips = n_row // 2
    head_rows = width // n_row
    head_cols = width // n_col
    bounds = [0, width // 8, width // 4, width // 2, width]
    row = lax.axis_index("row")
    col = lax.axis_index("col")
    chip = row // 2
    core = row % 2

    side = chip % 2
    level = chip // 2

    def peer(k, e):
        there = chip + (k % 2) * (1 - 2 * side) + (k // 2) * (2 - 4 * level)
        return there * 2 + (core if e == 0 else 1 - core)

    barrier = pltpu.get_barrier_semaphore()
    for d in range(1, n_row):
        pl.semaphore_signal(
            barrier, inc=1, device_id=((row + d) % n_row, col), device_id_type=MESH
        )
    for d in range(1, n_col):
        pl.semaphore_signal(
            barrier, inc=1, device_id=(row, (col + d) % n_col), device_id_type=MESH
        )

    def remote(src, dst, send, recv, device):
        return pltpu.make_async_remote_copy(
            src_ref=src,
            dst_ref=dst,
            send_sem=send,
            recv_sem=recv,
            device_id=device,
            device_id_type=MESH,
        )

    behind_copy = remote(
        text_ref, text_behind, near_send.at[0], near_recv.at[0], ((row + 1) % n_row, col)
    )
    ahead_copy = remote(
        pooled_ref,
        pooled_ahead,
        near_send.at[1],
        near_recv.at[1],
        ((row + n_row - 1) % n_row, col),
    )
    pl.semaphore_wait(barrier, n_row + n_col - 2)
    behind_copy.start()

    for tile in range(width // LANES):
        lanes = pl.ds(tile * LANES, LANES)
        pooled_t[lanes, :] = pooled_ref[:, lanes].T
    pool_copies = []
    for k in range(chips):
        for e in range(2):
            slot = 2 * k + e
            if slot == 0:
                continue
            target = peer(k, e)
            copy = remote(
                pooled_t.at[pl.ds(pl.multiple_of(target * head_rows, 16), head_rows), :],
                pooled_cols.at[:, pl.ds(slot * rows, rows)],
                pool_send.at[slot],
                pool_recv.at[slot],
                (target, col),
            )
            pool_copies.append(copy)
    pooled_cols[:, pl.ds(0, rows)] = pooled_t[
        pl.ds(pl.multiple_of(row * head_rows, 16), head_rows), :
    ]

    def fill_embed(source):
        at = 0
        for q in range(4):
            start, stop = aligned(bounds[q], bounds[q + 1])
            at += stop - start
        step = 3 * LANES if width % (3 * LANES) == 0 else LANES
        for base in range(0, width, step):
            part = dot_nn(source[...], weight_ref[:, pl.ds(base, step)])
            embed[:, pl.ds(base, step)] = part.astype(jnp.bfloat16)
        at = 0
        for q in range(4):
            start, stop = aligned(bounds[q], bounds[q + 1])
            part = embed[:, pl.ds(start, stop - start)].astype(jnp.float32)
            lane = lax.broadcasted_iota(jnp.int32, part.shape, 1) + start
            keep = (lane >= bounds[q]) & (lane < bounds[q + 1])
            masked[:, pl.ds(at, stop - start)] = jnp.where(keep, part, 0.0).astype(
                jnp.bfloat16
            )
            at += stop - start

    def masked_part(q):
        at = 0
        for before in range(q):
            start, stop = aligned(bounds[before], bounds[before + 1])
            at += stop - start
        start, stop = aligned(bounds[q], bounds[q + 1])
        return masked[:, pl.ds(at, stop - start)]

    def text_part(ref, q):
        start, stop = aligned(bounds[q], bounds[q + 1])
        return ref[:, pl.ds(start, stop - start)]

    fill_embed(pooled_ref)
    for copy in pool_copies:
        copy.start()
    text_id = lax.broadcasted_iota(jnp.int32, (rows, rows), 0)
    positive = (text_id == partner_ref[...]).astype(jnp.float32).T
    own = weights_of(
        lambda q: dot_nt(masked_part(q), text_part(text_ref, q)),
        positive,
        scale_ref,
        bias_ref,
        factor,
    )
    behind_copy.wait_recv()
    ahead_copy.start()
    cross = weights_of(
        lambda q: dot_nt(masked_part(q), text_part(text_behind, q)),
        None,
        scale_ref,
        bias_ref,
        factor,
    )

    def image_piece(q, start, stop):
        lanes = pl.ds(start, stop - start)
        return dot_nn(own[q], text_ref[:, lanes]) + dot_nn(cross[q], text_behind[:, lanes])

    def store_image(base, value):
        image[pl.ds(0, rows), pl.ds(base, LANES)] = value.astype(jnp.bfloat16)

    by_tile(image_piece, bounds, store_image)

    chunk = width // chunks
    half = rows // 2
    flip = (2 * col >= n_col).astype(jnp.int32)

    def mirrored(index, count):
        return flip * index + (1 - flip) * (count - 1 - index)

    def piece_of(slot, i, first=0, count=rows):
        lanes = pl.ds(pl.multiple_of(mirrored(i, chunks) * chunk, LANES), chunk)
        return image.at[pl.ds(slot * rows + first, count), lanes]

    image_copies = {}

    def send_image(name, src_slot, dst_slot, i, target, first=0, count=rows):
        image_copies[name, i] = remote(
            piece_of(src_slot, i, first, count),
            piece_of(dst_slot, i, first, count),
            image_send.at[name, i],
            image_recv.at[name, i],
            (target, col),
        )
        image_copies[name, i].start()

    def send_own(i):
        send_image(2, 0, 2, i, peer(1, 0))
        send_image(4, 0, 4, i, peer(2, 0))
        send_image(1, 0, 1, i, peer(0, 1))

    def pass_direct(i):
        image_copies[2, i].wait_recv()
        send_image(6, 2, 6, i, peer(2, 0), 0, half)
        send_image(3, 2, 3, i, peer(0, 1))
        image_copies[4, i].wait_recv()
        send_image(8, 4, 6, i, peer(1, 0), half, half)
        send_image(5, 4, 5, i, peer(0, 1))

    def pass_corner(i):
        image_copies[6, i].wait_recv()
        image_copies[8, i].wait_recv()
        send_image(7, 6, 7, i, peer(0, 1))

    for i in range(chunks - 1):
        send_own(i)

    def own_text_piece(q, start, stop):
        return dot_nn(own[q].T, embed[:, pl.ds(start, stop - start)])

    def store_text(base, value):
        text_grad_ref[:, pl.ds(base, LANES)] = value

    by_tile(own_text_piece, bounds, store_text)

    pass_direct(0)
    send_own(chunks - 1)
    ahead_copy.wait_recv()
    fill_embed(pooled_ahead)
    pass_corner(0)
    for i in range(1, chunks):
        pass_direct(i)
    ahead = weights_of(
        lambda q: dot_nt(text_part(text_ref, q), masked_part(q)),
        None,
        scale_ref,
        bias_ref,
        factor,
    )

    def ahead_piece(q, start, stop):
        return dot_nn(ahead[q], embed[:, pl.ds(start, stop - start)])

    def add_text(base, value):
        lanes = pl.ds(base, LANES)
        text_grad_ref[:, lanes] = text_grad_ref[:, lanes] + value

    main = head_cols // LANES * LANES
    tail = head_cols - main
    groups = head_rows // tail_rows

    def lanes_of(block):
        first = block * head_cols // LANES * LANES
        offset = block * head_cols - first
        part = total[:, pl.ds(pl.multiple_of(first, LANES), window)]
        return pltpu.roll(part, (window - offset) % window, 1)

    def packed(block):
        part = lanes_of(block)
        parts = [part[:, base : base + LANES] for base in range(0, main, LANES)]
        if tail:
            last = part[:, main : main + LANES]
            lane = lax.broadcasted_iota(jnp.int32, last.shape, 1)
            last = jnp.where(lane < tail, last, 0.0)
            joined = last[:tail_rows]
            for j in range(1, groups):
                here = last[j * tail_rows : (j + 1) * tail_rows]
                joined = joined + pltpu.roll(here, j * tail, 1)
            parts.append(joined)
        return parts

    def out_copy(block):
        return remote(
            sent.at[block],
            landed.at[col],
            out_send.at[block],
            out_recv.at[col],
            (row, block),
        )

    def in_copy(block):
        return remote(
            sent.at[block],
            landed.at[block],
            out_send.at[block],
            out_recv.at[block],
            (row, block),
        )

    for copy in pool_copies:
        copy.wait_recv()
    done = 0
    for i in range(chunks):
        if i > 0:
            pass_corner(i)
        image_copies[1, i].wait_recv()
        for slot in (3, 5, 7):
            image_copies[slot, i].wait_recv()
        lanes = pl.ds(pl.multiple_of(mirrored(i, chunks) * chunk, LANES), chunk)
        total[:, lanes] = dot_nn(pooled_cols[...], image[:, lanes])
        while done < n_col and ready[done] <= (i + 1) * chunk:
            block = mirrored(done, n_col)

            @pl.when(block != col)
            def _():
                at = 0
                for part in packed(block):
                    count = part.shape[0]
                    sent[block, pl.ds(at, count), :] = part.astype(jnp.bfloat16)
                    at += count
                out_copy(block).start()

            done += 1
        if i == 0:
            by_tile(ahead_piece, bounds, add_text)

    results = packed(col)
    for d in range(n_col - 1, 0, -1):
        block = (col + d) % n_col
        in_copy(block).wait_recv()
        at = 0
        for n, part in enumerate(results):
            count = part.shape[0]
            got = landed[block, pl.ds(at, count), :]
            results[n] = part + got.astype(jnp.float32)
            at += count
    for n in range(main // LANES):
        head_grad_ref[:, pl.ds(n * LANES, LANES)] = results[n]
    if tail:
        for j in range(groups):
            here = results[-1]
            if j > 0:
                here = pltpu.roll(here, LANES - j * tail, 1)
            head_grad_ref[pl.ds(j * tail_rows, tail_rows), pl.ds(main, tail)] = here[:, :tail]

    behind_copy.wait_send()
    ahead_copy.wait_send()
    for copy in pool_copies:
        copy.wait_send()
    for name in sorted(image_copies):
        image_copies[name].wait_send()
    for d in range(1, n_col):
        in_copy((col + d) % n_col).wait_send()


def plan_of(width, n_row, n_col):
    head_rows, head_cols = width // n_row, width // n_col
    chunks = next((n for n in (3, 2, 1) if width % (n * LANES) == 0), None)
    spans = [aligned(c * head_cols, (c + 1) * head_cols) for c in range(n_col)]
    window = max(stop - start for start, stop in spans)
    starts = [start for start, _ in spans]
    if chunks is None or any(start + window > width for start in starts):
        return None
    ready = [
        max(starts[c] + window, width - starts[n_col - 1 - c]) for c in range(n_col)
    ]
    tail = head_cols % LANES
    fitting = [
        n
        for n in range(1, LANES // tail + 1 if tail else 2)
        if head_rows % (16 * n) == 0
    ]
    if not fitting or head_cols < LANES:
        return None
    return chunks, ready, window, head_rows // max(fitting)


def fused_body(n_row, n_col, pooled, text_embed, head_weight, logit_scale, logit_bias, partner):
    rows, width = pooled.shape
    factor = 1.0 / math.sqrt(rows * n_row * n_col)
    chunks, ready, window, tail_rows = plan_of(width, n_row, n_col)
    head_cols = width // n_col
    packed_rows = head_cols // LANES * (width // n_row)
    packed_rows += tail_rows if head_cols % LANES else 0
    bounds = [0, width // 8, width // 4, width // 2, width]
    spans = [aligned(bounds[q], bounds[q + 1]) for q in range(4)]
    masked_width = sum(stop - start for start, stop in spans)
    head_rows, head_cols = width // n_row, width // n_col
    vmem = pl.BlockSpec(memory_space=pltpu.VMEM)
    smem = pl.BlockSpec(memory_space=pltpu.SMEM)
    dma = pltpu.SemaphoreType.DMA
    return pl.pallas_call(
        functools.partial(
            kernel, n_row, n_col, factor, chunks, ready, window, tail_rows
        ),
        out_shape=(
            jax.ShapeDtypeStruct((rows, width), jnp.float32),
            jax.ShapeDtypeStruct((head_rows, head_cols), jnp.float32),
        ),
        in_specs=[vmem, vmem, vmem, smem, smem, vmem],
        out_specs=(vmem, vmem),
        scratch_shapes=[
            pltpu.VMEM((rows, width), jnp.bfloat16),
            pltpu.VMEM((rows, width), jnp.bfloat16),
            pltpu.VMEM((width, rows), jnp.bfloat16),
            pltpu.VMEM((head_rows, n_row * rows), jnp.bfloat16),
            pltpu.VMEM((rows, width), jnp.bfloat16),
            pltpu.VMEM((rows, masked_width), jnp.bfloat16),
            pltpu.VMEM((n_row * rows, width), jnp.bfloat16),
            pltpu.VMEM((head_rows, width), jnp.float32),
            pltpu.VMEM((n_col, packed_rows, LANES), jnp.bfloat16),
            pltpu.VMEM((n_col, packed_rows, LANES), jnp.bfloat16),
            dma((2,)),
            dma((2,)),
            dma((n_row,)),
            dma((n_row,)),
            dma((n_row + 1, chunks)),
            dma((n_row + 1, chunks)),
            dma((n_col,)),
            dma((n_col,)),
        ],
        compiler_params=pltpu.CompilerParams(collective_id=0, has_side_effects=True),
    )(pooled, text_embed, head_weight, logit_scale, logit_bias, partner)


def per_device(n_row, n_col):
    def run(pooled, text_embed, head_weight, logit_scale, logit_bias, partner):
        rows, width = pooled.shape
        fused = (
            n_row == 2**3
            and n_col > 1
            and rows == LANES
            and width % LANES == 0
            and width % (16 * n_row) == 0
            and width % n_col == 0
            and plan_of(width, n_row, n_col) is not None
        )
        args = (pooled, text_embed, head_weight, logit_scale, logit_bias, partner)
        return fused_body(n_row, n_col, *args) if fused else body(*args)

    return run


def solution(mesh):
    in_specs = (
        P(("row", "col"), None),
        P(("row", "col"), None),
        P(),
        P(),
        P(),
        P(("row", "col"), None),
    )
    out_specs = (P(("row", "col"), None), P("row", "col"))
    run = per_device(mesh.shape["row"], mesh.shape["col"])
    return jax.shard_map(run, mesh=mesh, in_specs=in_specs, out_specs=out_specs, check_vma=False)
```

```python
import functools
import math

import jax
import jax.numpy as jnp
from jax import lax
from jax.experimental import pallas as pl
from jax.experimental.pallas import tpu as pltpu
from jax.sharding import PartitionSpec as P

LANES = 128
MESH = pl.DeviceIdType.MESH


def shifted(value, axis, by):
    count = lax.axis_size(axis)
    return lax.ppermute(value, axis, [(i, (i + by) % count) for i in range(count)])


def segment_weights(image_part, text_part, positive, logit_scale, logit_bias, factor):
    model_width = image_part.shape[1]
    bounds = [0, model_width // 8, model_width // 4, model_width // 2, model_width]
    running = jnp.zeros((image_part.shape[0], text_part.shape[0]), jnp.float32)
    level_grads = []
    for prefix in range(4):
        low_end = bounds[prefix]
        high_end = bounds[prefix + 1]
        running = running + jnp.dot(
            image_part[:, low_end:high_end],
            text_part[:, low_end:high_end].T,
            preferred_element_type=jnp.float32,
        )
        logits = logit_scale[prefix] * running + logit_bias[prefix]
        level_grads.append((jax.nn.sigmoid(logits) - positive) * factor)
    weights = []
    carried = jnp.zeros_like(running)
    for prefix in range(3, -1, -1):
        carried = carried + logit_scale[prefix] * level_grads[prefix]
        weights.insert(0, carried.astype(jnp.bfloat16))
    return (weights, bounds)


def image_side(weights, bounds, text_part):
    pieces = []
    for prefix in range(4):
        pieces.append(
            jnp.dot(
                weights[prefix],
                text_part[:, bounds[prefix] : bounds[prefix + 1]],
                preferred_element_type=jnp.float32,
            )
        )
    return jnp.concatenate(pieces, 1)


def text_side(weights, bounds, image_part):
    pieces = []
    for prefix in range(4):
        pieces.append(
            jnp.dot(
                weights[prefix].T,
                image_part[:, bounds[prefix] : bounds[prefix + 1]],
                preferred_element_type=jnp.float32,
            )
        )
    return jnp.concatenate(pieces, 1)


def body(pooled, text_embed, head_weight, logit_scale, logit_bias, partner):
    block_rows = pooled.shape[0]
    factor = 1.0 / math.sqrt(block_rows * lax.axis_size("row") * lax.axis_size("col"))
    embedding = jnp.dot(pooled, head_weight, preferred_element_type=jnp.float32).astype(
        jnp.bfloat16
    )
    local_ids = jnp.arange(block_rows, dtype=jnp.int32)
    positive = (partner[0][:, None] == local_ids[None, :]).astype(jnp.float32)
    empty = jnp.zeros((block_rows, block_rows), jnp.float32)
    weights, bounds = segment_weights(
        embedding, text_embed, positive, logit_scale, logit_bias, factor
    )
    own_image = image_side(weights, bounds, text_embed)
    own_text = text_side(weights, bounds, embedding)
    behind = shifted(text_embed, "row", 1)
    weights, bounds = segment_weights(embedding, behind, empty, logit_scale, logit_bias, factor)
    cross_image = image_side(weights, bounds, behind)
    cross_text = text_side(weights, bounds, embedding)
    returned = shifted(cross_text.astype(jnp.bfloat16), "row", -1).astype(cross_text.dtype)
    text_grad = own_text + returned
    image_grad = own_image + cross_image
    column_block = lax.all_to_all(
        image_grad.astype(jnp.bfloat16), "col", split_axis=1, concat_axis=0, tiled=True
    ).astype(image_grad.dtype)
    group_rows = lax.all_gather(pooled, "col", axis=0, tiled=True)
    block_term = jnp.dot(
        group_rows.astype(jnp.float32).T, column_block, precision=lax.Precision.HIGHEST
    )
    head_grad = lax.psum_scatter(block_term, "row", scatter_dimension=0, tiled=True)
    return (text_grad, head_grad)


def dot_nt(left, right):
    return lax.dot_general(
        left, right, (((1,), (1,)), ((), ())), preferred_element_type=jnp.float32
    )


def dot_nn(left, right):
    return jnp.dot(left, right, preferred_element_type=jnp.float32)


def aligned(low_end, high_end):
    return low_end // LANES * LANES, -(-high_end // LANES) * LANES


def weights_of(score_of, positive, scale_ref, bias_ref, factor):
    running = None
    level_grads = []
    for prefix in range(4):
        part = score_of(prefix)
        running = part if running is None else running + part
        gate = jax.nn.sigmoid(scale_ref[prefix] * running + bias_ref[prefix])
        if positive is not None:
            gate = gate - positive
        level_grads.append(gate * factor)
    weights = [None] * 4
    carried = None
    for prefix in range(3, -1, -1):
        term = scale_ref[prefix] * level_grads[prefix]
        carried = term if carried is None else carried + term
        weights[prefix] = carried.astype(jnp.bfloat16)
    return weights


def by_tile(piece_of, bounds, store):
    pieces = []
    for q in range(4):
        start, stop = aligned(bounds[q], bounds[q + 1])
        pieces.append((start, stop, piece_of(q, start, stop)))
    for tile in range(bounds[4] // LANES):
        base = tile * LANES
        value = None
        for q in range(4):
            start, stop, piece = pieces[q]
            if start <= base < stop:
                here = piece[:, base - start : base - start + LANES]
                if value is None:
                    value = here
                else:
                    lane = lax.broadcasted_iota(jnp.int32, here.shape, 1)
                    value = jnp.where(lane < bounds[q] - base, value, here)
        store(base, value)


def kernel(
    n_row,
    n_col,
    factor,
    chunks,
    ready,
    window,
    tail_rows,
    pooled_ref,
    text_ref,
    weight_hbm,
    scale_ref,
    bias_ref,
    partner_ref,
    text_grad_ref,
    head_grad_ref,
    weight_ref,
    weight_sem,
    image_own,
    pooled_ahead,
    text_behind,
    pooled_t,
    pooled_cols,
    embed,
    masked,
    image,
    total,
    sent,
    landed,
    near_send,
    near_recv,
    pool_send,
    pool_recv,
    image_send,
    image_recv,
    out_send,
    out_recv,
):
    rows, width = pooled_ref.shape
    chips = n_row // 2
    head_rows = width // n_row
    head_cols = width // n_col
    bounds = [0, width // 8, width // 4, width // 2, width]
    row = lax.axis_index("row")
    col = lax.axis_index("col")
    chip = row // 2
    core = row % 2

    side = chip % 2
    level = chip // 2

    def peer(k, e):
        there = chip + (k % 2) * (1 - 2 * side) + (k // 2) * (2 - 4 * level)
        return there * 2 + (core if e == 0 else 1 - core)

    weight_copy = pltpu.make_async_copy(weight_hbm, weight_ref, weight_sem)
    weight_copy.start()

    barrier = pltpu.get_barrier_semaphore()
    for d in range(1, n_row):
        pl.semaphore_signal(
            barrier, inc=1, device_id=((row + d) % n_row, col), device_id_type=MESH
        )
    for d in range(1, n_col):
        pl.semaphore_signal(
            barrier, inc=1, device_id=(row, (col + d) % n_col), device_id_type=MESH
        )

    def remote(src, dst, send, recv, device):
        return pltpu.make_async_remote_copy(
            src_ref=src,
            dst_ref=dst,
            send_sem=send,
            recv_sem=recv,
            device_id=device,
            device_id_type=MESH,
        )

    behind_copy = remote(
        text_ref, text_behind, near_send.at[0], near_recv.at[0], ((row + 1) % n_row, col)
    )
    ahead_copy = remote(
        pooled_ref,
        pooled_ahead,
        near_send.at[1],
        near_recv.at[1],
        ((row + n_row - 1) % n_row, col),
    )
    pl.semaphore_wait(barrier, n_row + n_col - 2)
    behind_copy.start()

    for tile in range(width // LANES):
        lanes = pl.ds(tile * LANES, LANES)
        pooled_t[lanes, :] = pooled_ref[:, lanes].T
    pool_copies = []
    for k in range(chips):
        for e in range(2):
            slot = 2 * k + e
            if slot == 0:
                continue
            target = peer(k, e)
            copy = remote(
                pooled_t.at[pl.ds(pl.multiple_of(target * head_rows, 16), head_rows), :],
                pooled_cols.at[:, pl.ds(slot * rows, rows)],
                pool_send.at[slot],
                pool_recv.at[slot],
                (target, col),
            )
            pool_copies.append(copy)
    pooled_cols[:, pl.ds(0, rows)] = pooled_t[
        pl.ds(pl.multiple_of(row * head_rows, 16), head_rows), :
    ]

    def fill_embed(source):
        at = 0
        for q in range(4):
            start, stop = aligned(bounds[q], bounds[q + 1])
            at += stop - start
        step = 3 * LANES if width % (3 * LANES) == 0 else LANES
        for base in range(0, width, step):
            part = dot_nn(source[...], weight_ref[:, pl.ds(base, step)])
            embed[:, pl.ds(base, step)] = part.astype(jnp.bfloat16)
        at = 0
        for q in range(4):
            start, stop = aligned(bounds[q], bounds[q + 1])
            part = embed[:, pl.ds(start, stop - start)].astype(jnp.float32)
            lane = lax.broadcasted_iota(jnp.int32, part.shape, 1) + start
            keep = (lane >= bounds[q]) & (lane < bounds[q + 1])
            masked[:, pl.ds(at, stop - start)] = jnp.where(keep, part, 0.0).astype(
                jnp.bfloat16
            )
            at += stop - start

    def masked_part(q):
        at = 0
        for before in range(q):
            start, stop = aligned(bounds[before], bounds[before + 1])
            at += stop - start
        start, stop = aligned(bounds[q], bounds[q + 1])
        return masked[:, pl.ds(at, stop - start)]

    def text_part(ref, q):
        start, stop = aligned(bounds[q], bounds[q + 1])
        return ref[:, pl.ds(start, stop - start)]

    weight_copy.wait()
    fill_embed(pooled_ref)
    for copy in pool_copies:
        copy.start()
    text_id = lax.broadcasted_iota(jnp.int32, (rows, rows), 0)
    positive = (text_id == partner_ref[...]).astype(jnp.float32).T
    own = weights_of(
        lambda q: dot_nt(masked_part(q), text_part(text_ref, q)),
        positive,
        scale_ref,
        bias_ref,
        factor,
    )

    def own_image_piece(q, start, stop):
        return dot_nn(own[q], text_ref[:, pl.ds(start, stop - start)])

    def keep_image(base, value):
        image_own[:, pl.ds(base, LANES)] = value

    by_tile(own_image_piece, bounds, keep_image)

    def own_text_piece(q, start, stop):
        return dot_nn(own[q].T, embed[:, pl.ds(start, stop - start)])

    def store_text(base, value):
        text_grad_ref[:, pl.ds(base, LANES)] = value

    by_tile(own_text_piece, bounds, store_text)

    behind_copy.wait_recv()
    cross = weights_of(
        lambda q: dot_nt(masked_part(q), text_part(text_behind, q)),
        None,
        scale_ref,
        bias_ref,
        factor,
    )

    def image_piece(q, start, stop):
        lanes = pl.ds(start, stop - start)
        return dot_nn(cross[q], text_behind[:, lanes])

    def store_image(base, value):
        lanes = pl.ds(base, LANES)
        image[pl.ds(0, rows), lanes] = (image_own[:, lanes] + value).astype(jnp.bfloat16)

    by_tile(image_piece, bounds, store_image)

    chunk = width // chunks
    half = rows // 2
    flip = (2 * col >= n_col).astype(jnp.int32)

    def mirrored(index, count):
        return flip * index + (1 - flip) * (count - 1 - index)

    def piece_of(slot, i, first=0, count=rows):
        lanes = pl.ds(pl.multiple_of(mirrored(i, chunks) * chunk, LANES), chunk)
        return image.at[pl.ds(slot * rows + first, count), lanes]

    image_copies = {}

    def send_image(name, src_slot, dst_slot, i, target, first=0, count=rows):
        image_copies[name, i] = remote(
            piece_of(src_slot, i, first, count),
            piece_of(dst_slot, i, first, count),
            image_send.at[name, i],
            image_recv.at[name, i],
            (target, col),
        )
        image_copies[name, i].start()

    def send_own(i):
        send_image(2, 0, 2, i, peer(1, 0))
        send_image(4, 0, 4, i, peer(2, 0))
        send_image(1, 0, 1, i, peer(0, 1))

    def pass_direct(i):
        image_copies[2, i].wait_recv()
        send_image(6, 2, 6, i, peer(2, 0), 0, half)
        send_image(3, 2, 3, i, peer(0, 1))
        image_copies[4, i].wait_recv()
        send_image(8, 4, 6, i, peer(1, 0), half, half)
        send_image(5, 4, 5, i, peer(0, 1))

    def pass_corner(i):
        image_copies[6, i].wait_recv()
        image_copies[8, i].wait_recv()
        send_image(7, 6, 7, i, peer(0, 1))

    for i in range(chunks - 1):
        send_own(i)

    pass_direct(0)
    send_own(chunks - 1)
    pass_corner(0)
    ahead_copy.start()
    for i in range(1, chunks):
        pass_direct(i)
    for i in range(1, chunks - 1):
        pass_corner(i)

    main = head_cols // LANES * LANES
    tail = head_cols - main
    groups = head_rows // tail_rows

    def lanes_of(block):
        first = block * head_cols // LANES * LANES
        offset = block * head_cols - first
        part = total[:, pl.ds(pl.multiple_of(first, LANES), window)]
        return pltpu.roll(part, (window - offset) % window, 1)

    def packed(block):
        part = lanes_of(block)
        parts = [part[:, base : base + LANES] for base in range(0, main, LANES)]
        if tail:
            last = part[:, main : main + LANES]
            lane = lax.broadcasted_iota(jnp.int32, last.shape, 1)
            last = jnp.where(lane < tail, last, 0.0)
            joined = last[:tail_rows]
            for j in range(1, groups):
                here = last[j * tail_rows : (j + 1) * tail_rows]
                joined = joined + pltpu.roll(here, j * tail, 1)
            parts.append(joined)
        return parts

    def out_copy(block):
        return remote(
            sent.at[block],
            landed.at[col],
            out_send.at[block],
            out_recv.at[col],
            (row, block),
        )

    def in_copy(block):
        return remote(
            sent.at[block],
            landed.at[block],
            out_send.at[block],
            out_recv.at[block],
            (row, block),
        )

    for copy in pool_copies:
        copy.wait_recv()
    done = 0
    for i in range(chunks):
        if i == chunks - 1:
            pass_corner(i)
        image_copies[1, i].wait_recv()
        for slot in (3, 5, 7):
            image_copies[slot, i].wait_recv()
        lanes = pl.ds(pl.multiple_of(mirrored(i, chunks) * chunk, LANES), chunk)
        total[:, lanes] = dot_nn(pooled_cols[...], image[:, lanes])
        while done < n_col and ready[done] <= (i + 1) * chunk:
            block = mirrored(done, n_col)

            @pl.when(block != col)
            def _():
                at = 0
                for part in packed(block):
                    count = part.shape[0]
                    sent[block, pl.ds(at, count), :] = part.astype(jnp.bfloat16)
                    at += count
                out_copy(block).start()

            done += 1

    ahead_copy.wait_recv()
    fill_embed(pooled_ahead)
    ahead = weights_of(
        lambda q: dot_nt(text_part(text_ref, q), masked_part(q)),
        None,
        scale_ref,
        bias_ref,
        factor,
    )

    def ahead_piece(q, start, stop):
        return dot_nn(ahead[q], embed[:, pl.ds(start, stop - start)])

    def add_text(base, value):
        lanes = pl.ds(base, LANES)
        text_grad_ref[:, lanes] = text_grad_ref[:, lanes] + value

    by_tile(ahead_piece, bounds, add_text)

    results = packed(col)
    for d in range(n_col - 1, 0, -1):
        block = (col + d) % n_col
        in_copy(block).wait_recv()
        at = 0
        for n, part in enumerate(results):
            count = part.shape[0]
            got = landed[block, pl.ds(at, count), :]
            results[n] = part + got.astype(jnp.float32)
            at += count
    for n in range(main // LANES):
        head_grad_ref[:, pl.ds(n * LANES, LANES)] = results[n]
    if tail:
        for j in range(groups):
            here = results[-1]
            if j > 0:
                here = pltpu.roll(here, LANES - j * tail, 1)
            head_grad_ref[pl.ds(j * tail_rows, tail_rows), pl.ds(main, tail)] = here[:, :tail]

    behind_copy.wait_send()
    ahead_copy.wait_send()
    for copy in pool_copies:
        copy.wait_send()
    for name in sorted(image_copies):
        image_copies[name].wait_send()
    for d in range(1, n_col):
        in_copy((col + d) % n_col).wait_send()


def deliver(text_grad, head_grad):
    parts = 4
    step = text_grad.shape[0] // parts

    def move(text_from, head_from, text_to, head_to, text_held, head_held, sems, head_sems):
        def rows_of(ref, n):
            return ref.at[pl.ds(n * step, step), :]

        loads = [
            pltpu.make_async_copy(rows_of(text_from, n), rows_of(text_held, n), sems.at[0, n])
            for n in range(parts)
        ]
        head_load = pltpu.make_async_copy(head_from, head_held, head_sems.at[0])
        for load in loads:
            load.start()
        head_load.start()
        stores = []
        for n in range(parts):
            loads[n].wait()
            stores.append(
                pltpu.make_async_copy(rows_of(text_held, n), rows_of(text_to, n), sems.at[1, n])
            )
            stores[n].start()
        head_load.wait()
        head_store = pltpu.make_async_copy(head_held, head_to, head_sems.at[1])
        head_store.start()
        for store in stores:
            store.wait()
        head_store.wait()

    anywhere = pl.BlockSpec(memory_space=pl.ANY)
    return pl.pallas_call(
        move,
        out_shape=(
            jax.ShapeDtypeStruct(text_grad.shape, text_grad.dtype),
            jax.ShapeDtypeStruct(head_grad.shape, head_grad.dtype),
        ),
        in_specs=[anywhere, anywhere],
        out_specs=(anywhere, anywhere),
        scratch_shapes=[
            pltpu.VMEM(text_grad.shape, text_grad.dtype),
            pltpu.VMEM(head_grad.shape, head_grad.dtype),
            pltpu.SemaphoreType.DMA((2, parts)),
            pltpu.SemaphoreType.DMA((2,)),
        ],
    )(text_grad, head_grad)


def plan_of(width, n_row, n_col):
    head_rows, head_cols = width // n_row, width // n_col
    chunks = next((n for n in (3, 2, 1) if width % (n * LANES) == 0), None)
    spans = [aligned(c * head_cols, (c + 1) * head_cols) for c in range(n_col)]
    window = max(stop - start for start, stop in spans)
    starts = [start for start, _ in spans]
    if chunks is None or any(start + window > width for start in starts):
        return None
    ready = [
        max(starts[c] + window, width - starts[n_col - 1 - c]) for c in range(n_col)
    ]
    tail = head_cols % LANES
    fitting = [
        n
        for n in range(1, LANES // tail + 1 if tail else 2)
        if head_rows % (16 * n) == 0
    ]
    if not fitting or head_cols < LANES:
        return None
    return chunks, ready, window, head_rows // max(fitting)


def fused_body(n_row, n_col, pooled, text_embed, head_weight, logit_scale, logit_bias, partner):
    rows, width = pooled.shape
    factor = 1.0 / math.sqrt(rows * n_row * n_col)
    chunks, ready, window, tail_rows = plan_of(width, n_row, n_col)
    head_cols = width // n_col
    packed_rows = head_cols // LANES * (width // n_row)
    packed_rows += tail_rows if head_cols % LANES else 0
    bounds = [0, width // 8, width // 4, width // 2, width]
    spans = [aligned(bounds[q], bounds[q + 1]) for q in range(4)]
    masked_width = sum(stop - start for start, stop in spans)
    head_rows, head_cols = width // n_row, width // n_col
    vmem = pl.BlockSpec(memory_space=pltpu.VMEM)
    smem = pl.BlockSpec(memory_space=pltpu.SMEM)
    dma = pltpu.SemaphoreType.DMA
    return pl.pallas_call(
        functools.partial(
            kernel, n_row, n_col, factor, chunks, ready, window, tail_rows
        ),
        out_shape=(
            jax.ShapeDtypeStruct((rows, width), jnp.float32),
            jax.ShapeDtypeStruct((head_rows, head_cols), jnp.float32),
        ),
        in_specs=[vmem, vmem, pl.BlockSpec(memory_space=pl.ANY), smem, smem, vmem],
        out_specs=(vmem, vmem),
        scratch_shapes=[
            pltpu.VMEM(head_weight.shape, jnp.bfloat16),
            dma,
            pltpu.VMEM((rows, width), jnp.float32),
            pltpu.VMEM((rows, width), jnp.bfloat16),
            pltpu.VMEM((rows, width), jnp.bfloat16),
            pltpu.VMEM((width, rows), jnp.bfloat16),
            pltpu.VMEM((head_rows, n_row * rows), jnp.bfloat16),
            pltpu.VMEM((rows, width), jnp.bfloat16),
            pltpu.VMEM((rows, masked_width), jnp.bfloat16),
            pltpu.VMEM((n_row * rows, width), jnp.bfloat16),
            pltpu.VMEM((head_rows, width), jnp.float32),
            pltpu.VMEM((n_col, packed_rows, LANES), jnp.bfloat16),
            pltpu.VMEM((n_col, packed_rows, LANES), jnp.bfloat16),
            dma((2,)),
            dma((2,)),
            dma((n_row,)),
            dma((n_row,)),
            dma((n_row + 1, chunks)),
            dma((n_row + 1, chunks)),
            dma((n_col,)),
            dma((n_col,)),
        ],
        compiler_params=pltpu.CompilerParams(collective_id=0, has_side_effects=True),
    )(pooled, text_embed, head_weight, logit_scale, logit_bias, partner)


def per_device(n_row, n_col):
    def run(pooled, text_embed, head_weight, logit_scale, logit_bias, partner):
        rows, width = pooled.shape
        fused = (
            n_row == 2**3
            and n_col > 1
            and rows == LANES
            and width % LANES == 0
            and width % (16 * n_row) == 0
            and width % n_col == 0
            and plan_of(width, n_row, n_col) is not None
        )
        args = (pooled, text_embed, head_weight, logit_scale, logit_bias, partner)
        return deliver(*fused_body(n_row, n_col, *args)) if fused else body(*args)

    return run


def solution(mesh):
    in_specs = (
        P(("row", "col"), None),
        P(("row", "col"), None),
        P(),
        P(),
        P(),
        P(("row", "col"), None),
    )
    out_specs = (P(("row", "col"), None), P("row", "col"))
    run = per_device(mesh.shape["row"], mesh.shape["col"])
    return jax.shard_map(run, mesh=mesh, in_specs=in_specs, out_specs=out_specs, check_vma=False)
```

```python
import functools
import math

import jax
import jax.numpy as jnp
from jax import lax
from jax.experimental import pallas as pl
from jax.experimental.pallas import tpu as pltpu
from jax.sharding import PartitionSpec as P

LANES = 128
MESH = pl.DeviceIdType.MESH


def shifted(value, axis, by):
    count = lax.axis_size(axis)
    return lax.ppermute(value, axis, [(i, (i + by) % count) for i in range(count)])


def segment_weights(image_part, text_part, positive, logit_scale, logit_bias, factor):
    model_width = image_part.shape[1]
    bounds = [0, model_width // 8, model_width // 4, model_width // 2, model_width]
    running = jnp.zeros((image_part.shape[0], text_part.shape[0]), jnp.float32)
    level_grads = []
    for prefix in range(4):
        low_end = bounds[prefix]
        high_end = bounds[prefix + 1]
        running = running + jnp.dot(
            image_part[:, low_end:high_end],
            text_part[:, low_end:high_end].T,
            preferred_element_type=jnp.float32,
        )
        logits = logit_scale[prefix] * running + logit_bias[prefix]
        level_grads.append((jax.nn.sigmoid(logits) - positive) * factor)
    weights = []
    carried = jnp.zeros_like(running)
    for prefix in range(3, -1, -1):
        carried = carried + logit_scale[prefix] * level_grads[prefix]
        weights.insert(0, carried.astype(jnp.bfloat16))
    return (weights, bounds)


def image_side(weights, bounds, text_part):
    pieces = []
    for prefix in range(4):
        pieces.append(
            jnp.dot(
                weights[prefix],
                text_part[:, bounds[prefix] : bounds[prefix + 1]],
                preferred_element_type=jnp.float32,
            )
        )
    return jnp.concatenate(pieces, 1)


def text_side(weights, bounds, image_part):
    pieces = []
    for prefix in range(4):
        pieces.append(
            jnp.dot(
                weights[prefix].T,
                image_part[:, bounds[prefix] : bounds[prefix + 1]],
                preferred_element_type=jnp.float32,
            )
        )
    return jnp.concatenate(pieces, 1)


def body(pooled, text_embed, head_weight, logit_scale, logit_bias, partner):
    block_rows = pooled.shape[0]
    factor = 1.0 / math.sqrt(block_rows * lax.axis_size("row") * lax.axis_size("col"))
    embedding = jnp.dot(pooled, head_weight, preferred_element_type=jnp.float32).astype(
        jnp.bfloat16
    )
    local_ids = jnp.arange(block_rows, dtype=jnp.int32)
    positive = (partner[0][:, None] == local_ids[None, :]).astype(jnp.float32)
    empty = jnp.zeros((block_rows, block_rows), jnp.float32)
    weights, bounds = segment_weights(
        embedding, text_embed, positive, logit_scale, logit_bias, factor
    )
    own_image = image_side(weights, bounds, text_embed)
    own_text = text_side(weights, bounds, embedding)
    behind = shifted(text_embed, "row", 1)
    weights, bounds = segment_weights(embedding, behind, empty, logit_scale, logit_bias, factor)
    cross_image = image_side(weights, bounds, behind)
    cross_text = text_side(weights, bounds, embedding)
    returned = shifted(cross_text.astype(jnp.bfloat16), "row", -1).astype(cross_text.dtype)
    text_grad = own_text + returned
    image_grad = own_image + cross_image
    column_block = lax.all_to_all(
        image_grad.astype(jnp.bfloat16), "col", split_axis=1, concat_axis=0, tiled=True
    ).astype(image_grad.dtype)
    group_rows = lax.all_gather(pooled, "col", axis=0, tiled=True)
    block_term = jnp.dot(
        group_rows.astype(jnp.float32).T, column_block, precision=lax.Precision.HIGHEST
    )
    head_grad = lax.psum_scatter(block_term, "row", scatter_dimension=0, tiled=True)
    return (text_grad, head_grad)


def dot_nt(left, right):
    return lax.dot_general(
        left, right, (((1,), (1,)), ((), ())), preferred_element_type=jnp.float32
    )


def dot_nn(left, right):
    return jnp.dot(left, right, preferred_element_type=jnp.float32)


def aligned(low_end, high_end):
    return low_end // LANES * LANES, -(-high_end // LANES) * LANES


def weights_of(score_of, positive, scale_ref, bias_ref, factor):
    running = None
    level_grads = []
    for prefix in range(4):
        part = score_of(prefix)
        running = part if running is None else running + part
        gate = jax.nn.sigmoid(scale_ref[prefix] * running + bias_ref[prefix])
        if positive is not None:
            gate = gate - positive
        level_grads.append(gate * factor)
    weights = [None] * 4
    carried = None
    for prefix in range(3, -1, -1):
        term = scale_ref[prefix] * level_grads[prefix]
        carried = term if carried is None else carried + term
        weights[prefix] = carried.astype(jnp.bfloat16)
    return weights


def by_tile(piece_of, bounds, store):
    pieces = []
    for q in range(4):
        start, stop = aligned(bounds[q], bounds[q + 1])
        pieces.append((start, stop, piece_of(q, start, stop)))
    for tile in range(bounds[4] // LANES):
        base = tile * LANES
        value = None
        for q in range(4):
            start, stop, piece = pieces[q]
            if start <= base < stop:
                here = piece[:, base - start : base - start + LANES]
                if value is None:
                    value = here
                else:
                    lane = lax.broadcasted_iota(jnp.int32, here.shape, 1)
                    value = jnp.where(lane < bounds[q] - base, value, here)
        store(base, value)


def kernel(
    n_row,
    n_col,
    factor,
    chunks,
    ready,
    window,
    tail_rows,
    pooled_ref,
    text_ref,
    weight_hbm,
    scale_ref,
    bias_ref,
    partner_ref,
    text_grad_ref,
    head_grad_ref,
    weight_ref,
    weight_sem,
    image_own,
    cross_text,
    text_back,
    text_behind,
    pooled_t,
    pooled_cols,
    embed,
    masked,
    image,
    total,
    sent,
    landed,
    near_send,
    near_recv,
    pool_send,
    pool_recv,
    image_send,
    image_recv,
    out_send,
    out_recv,
):
    rows, width = pooled_ref.shape
    chips = n_row // 2
    head_rows = width // n_row
    head_cols = width // n_col
    bounds = [0, width // 8, width // 4, width // 2, width]
    row = lax.axis_index("row")
    col = lax.axis_index("col")
    chip = row // 2
    core = row % 2

    side = chip % 2
    level = chip // 2

    def peer(k, e):
        there = chip + (k % 2) * (1 - 2 * side) + (k // 2) * (2 - 4 * level)
        return there * 2 + (core if e == 0 else 1 - core)

    weight_copy = pltpu.make_async_copy(weight_hbm, weight_ref, weight_sem)
    weight_copy.start()

    barrier = pltpu.get_barrier_semaphore()
    for d in range(1, n_row):
        pl.semaphore_signal(
            barrier, inc=1, device_id=((row + d) % n_row, col), device_id_type=MESH
        )
    for d in range(1, n_col):
        pl.semaphore_signal(
            barrier, inc=1, device_id=(row, (col + d) % n_col), device_id_type=MESH
        )

    def remote(src, dst, send, recv, device):
        return pltpu.make_async_remote_copy(
            src_ref=src,
            dst_ref=dst,
            send_sem=send,
            recv_sem=recv,
            device_id=device,
            device_id_type=MESH,
        )

    behind_copy = remote(
        text_ref, text_behind, near_send.at[0], near_recv.at[0], ((row + 1) % n_row, col)
    )
    back_copy = remote(
        cross_text,
        text_back,
        near_send.at[1],
        near_recv.at[1],
        ((row + n_row - 1) % n_row, col),
    )
    pl.semaphore_wait(barrier, n_row + n_col - 2)
    behind_copy.start()

    for tile in range(width // LANES):
        lanes = pl.ds(tile * LANES, LANES)
        pooled_t[lanes, :] = pooled_ref[:, lanes].T
    pool_copies = []
    for k in range(chips):
        for e in range(2):
            slot = 2 * k + e
            if slot == 0:
                continue
            target = peer(k, e)
            copy = remote(
                pooled_t.at[pl.ds(pl.multiple_of(target * head_rows, 16), head_rows), :],
                pooled_cols.at[:, pl.ds(slot * rows, rows)],
                pool_send.at[slot],
                pool_recv.at[slot],
                (target, col),
            )
            pool_copies.append(copy)
    pooled_cols[:, pl.ds(0, rows)] = pooled_t[
        pl.ds(pl.multiple_of(row * head_rows, 16), head_rows), :
    ]

    def fill_embed(source):
        at = 0
        for q in range(4):
            start, stop = aligned(bounds[q], bounds[q + 1])
            at += stop - start
        step = 3 * LANES if width % (3 * LANES) == 0 else LANES
        for base in range(0, width, step):
            part = dot_nn(source[...], weight_ref[:, pl.ds(base, step)])
            embed[:, pl.ds(base, step)] = part.astype(jnp.bfloat16)
        at = 0
        for q in range(4):
            start, stop = aligned(bounds[q], bounds[q + 1])
            part = embed[:, pl.ds(start, stop - start)].astype(jnp.float32)
            lane = lax.broadcasted_iota(jnp.int32, part.shape, 1) + start
            keep = (lane >= bounds[q]) & (lane < bounds[q + 1])
            masked[:, pl.ds(at, stop - start)] = jnp.where(keep, part, 0.0).astype(
                jnp.bfloat16
            )
            at += stop - start

    def masked_part(q):
        at = 0
        for before in range(q):
            start, stop = aligned(bounds[before], bounds[before + 1])
            at += stop - start
        start, stop = aligned(bounds[q], bounds[q + 1])
        return masked[:, pl.ds(at, stop - start)]

    def text_part(ref, q):
        start, stop = aligned(bounds[q], bounds[q + 1])
        return ref[:, pl.ds(start, stop - start)]

    weight_copy.wait()
    fill_embed(pooled_ref)
    for copy in pool_copies:
        copy.start()
    text_id = lax.broadcasted_iota(jnp.int32, (rows, rows), 0)
    positive = (text_id == partner_ref[...]).astype(jnp.float32).T
    own = weights_of(
        lambda q: dot_nt(masked_part(q), text_part(text_ref, q)),
        positive,
        scale_ref,
        bias_ref,
        factor,
    )

    def own_image_piece(q, start, stop):
        return dot_nn(own[q], text_ref[:, pl.ds(start, stop - start)])

    def keep_image(base, value):
        image_own[:, pl.ds(base, LANES)] = value

    by_tile(own_image_piece, bounds, keep_image)

    def own_text_piece(q, start, stop):
        return dot_nn(own[q].T, embed[:, pl.ds(start, stop - start)])

    def store_text(base, value):
        text_grad_ref[:, pl.ds(base, LANES)] = value

    by_tile(own_text_piece, bounds, store_text)

    behind_copy.wait_recv()
    cross = weights_of(
        lambda q: dot_nt(masked_part(q), text_part(text_behind, q)),
        None,
        scale_ref,
        bias_ref,
        factor,
    )

    def image_piece(q, start, stop):
        lanes = pl.ds(start, stop - start)
        return dot_nn(cross[q], text_behind[:, lanes])

    def store_image(base, value):
        lanes = pl.ds(base, LANES)
        image[pl.ds(0, rows), lanes] = (image_own[:, lanes] + value).astype(jnp.bfloat16)

    by_tile(image_piece, bounds, store_image)

    chunk = width // chunks
    half = rows // 2
    flip = (2 * col >= n_col).astype(jnp.int32)

    def mirrored(index, count):
        return flip * index + (1 - flip) * (count - 1 - index)

    def piece_of(slot, i, first=0, count=rows):
        lanes = pl.ds(pl.multiple_of(mirrored(i, chunks) * chunk, LANES), chunk)
        return image.at[pl.ds(slot * rows + first, count), lanes]

    image_copies = {}

    def send_image(name, src_slot, dst_slot, i, target, first=0, count=rows):
        image_copies[name, i] = remote(
            piece_of(src_slot, i, first, count),
            piece_of(dst_slot, i, first, count),
            image_send.at[name, i],
            image_recv.at[name, i],
            (target, col),
        )
        image_copies[name, i].start()

    def send_own(i):
        send_image(2, 0, 2, i, peer(1, 0))
        send_image(4, 0, 4, i, peer(2, 0))
        send_image(1, 0, 1, i, peer(0, 1))

    def pass_direct(i):
        image_copies[2, i].wait_recv()
        send_image(6, 2, 6, i, peer(2, 0), 0, half)
        send_image(3, 2, 3, i, peer(0, 1))
        image_copies[4, i].wait_recv()
        send_image(8, 4, 6, i, peer(1, 0), half, half)
        send_image(5, 4, 5, i, peer(0, 1))

    def pass_corner(i):
        image_copies[6, i].wait_recv()
        image_copies[8, i].wait_recv()
        send_image(7, 6, 7, i, peer(0, 1))

    for i in range(chunks - 1):
        send_own(i)

    def cross_text_piece(q, start, stop):
        return dot_nn(cross[q].T, embed[:, pl.ds(start, stop - start)])

    def store_cross(base, value):
        cross_text[:, pl.ds(base, LANES)] = value.astype(jnp.bfloat16)

    by_tile(cross_text_piece, bounds, store_cross)

    pass_direct(0)
    send_own(chunks - 1)
    pass_corner(0)
    back_copy.start()
    for i in range(1, chunks):
        pass_direct(i)
    for i in range(1, chunks - 1):
        pass_corner(i)

    main = head_cols // LANES * LANES
    tail = head_cols - main
    groups = head_rows // tail_rows

    def lanes_of(block):
        first = block * head_cols // LANES * LANES
        offset = block * head_cols - first
        part = total[:, pl.ds(pl.multiple_of(first, LANES), window)]
        return pltpu.roll(part, (window - offset) % window, 1)

    def packed(block):
        part = lanes_of(block)
        parts = [part[:, base : base + LANES] for base in range(0, main, LANES)]
        if tail:
            last = part[:, main : main + LANES]
            lane = lax.broadcasted_iota(jnp.int32, last.shape, 1)
            last = jnp.where(lane < tail, last, 0.0)
            joined = last[:tail_rows]
            for j in range(1, groups):
                here = last[j * tail_rows : (j + 1) * tail_rows]
                joined = joined + pltpu.roll(here, j * tail, 1)
            parts.append(joined)
        return parts

    def out_copy(block):
        return remote(
            sent.at[block],
            landed.at[col],
            out_send.at[block],
            out_recv.at[col],
            (row, block),
        )

    def in_copy(block):
        return remote(
            sent.at[block],
            landed.at[block],
            out_send.at[block],
            out_recv.at[block],
            (row, block),
        )

    for copy in pool_copies:
        copy.wait_recv()
    done = 0
    for i in range(chunks):
        if i == chunks - 1:
            pass_corner(i)
        image_copies[1, i].wait_recv()
        for slot in (3, 5, 7):
            image_copies[slot, i].wait_recv()
        lanes = pl.ds(pl.multiple_of(mirrored(i, chunks) * chunk, LANES), chunk)
        total[:, lanes] = dot_nn(pooled_cols[...], image[:, lanes])
        while done < n_col and ready[done] <= (i + 1) * chunk:
            block = mirrored(done, n_col)

            @pl.when(block != col)
            def _():
                at = 0
                for part in packed(block):
                    count = part.shape[0]
                    sent[block, pl.ds(at, count), :] = part.astype(jnp.bfloat16)
                    at += count
                out_copy(block).start()

            done += 1

    back_copy.wait_recv()
    text_grad_ref[...] = text_grad_ref[...] + text_back[...].astype(jnp.float32)

    results = packed(col)
    for d in range(n_col - 1, 0, -1):
        block = (col + d) % n_col
        in_copy(block).wait_recv()
        at = 0
        for n, part in enumerate(results):
            count = part.shape[0]
            got = landed[block, pl.ds(at, count), :]
            results[n] = part + got.astype(jnp.float32)
            at += count
    for n in range(main // LANES):
        head_grad_ref[:, pl.ds(n * LANES, LANES)] = results[n]
    if tail:
        for j in range(groups):
            here = results[-1]
            if j > 0:
                here = pltpu.roll(here, LANES - j * tail, 1)
            head_grad_ref[pl.ds(j * tail_rows, tail_rows), pl.ds(main, tail)] = here[:, :tail]

    behind_copy.wait_send()
    back_copy.wait_send()
    for copy in pool_copies:
        copy.wait_send()
    for name in sorted(image_copies):
        image_copies[name].wait_send()
    for d in range(1, n_col):
        in_copy((col + d) % n_col).wait_send()


def deliver(text_grad, head_grad):
    parts = 4
    step = text_grad.shape[0] // parts

    def move(text_from, head_from, text_to, head_to, text_held, head_held, sems, head_sems):
        def rows_of(ref, n):
            return ref.at[pl.ds(n * step, step), :]

        loads = [
            pltpu.make_async_copy(rows_of(text_from, n), rows_of(text_held, n), sems.at[0, n])
            for n in range(parts)
        ]
        head_load = pltpu.make_async_copy(head_from, head_held, head_sems.at[0])
        for load in loads:
            load.start()
        head_load.start()
        stores = []
        for n in range(parts):
            loads[n].wait()
            stores.append(
                pltpu.make_async_copy(rows_of(text_held, n), rows_of(text_to, n), sems.at[1, n])
            )
            stores[n].start()
        head_load.wait()
        head_store = pltpu.make_async_copy(head_held, head_to, head_sems.at[1])
        head_store.start()
        for store in stores:
            store.wait()
        head_store.wait()

    anywhere = pl.BlockSpec(memory_space=pl.ANY)
    return pl.pallas_call(
        move,
        out_shape=(
            jax.ShapeDtypeStruct(text_grad.shape, text_grad.dtype),
            jax.ShapeDtypeStruct(head_grad.shape, head_grad.dtype),
        ),
        in_specs=[anywhere, anywhere],
        out_specs=(anywhere, anywhere),
        scratch_shapes=[
            pltpu.VMEM(text_grad.shape, text_grad.dtype),
            pltpu.VMEM(head_grad.shape, head_grad.dtype),
            pltpu.SemaphoreType.DMA((2, parts)),
            pltpu.SemaphoreType.DMA((2,)),
        ],
    )(text_grad, head_grad)


def plan_of(width, n_row, n_col):
    head_rows, head_cols = width // n_row, width // n_col
    chunks = next((n for n in (3, 2, 1) if width % (n * LANES) == 0), None)
    spans = [aligned(c * head_cols, (c + 1) * head_cols) for c in range(n_col)]
    window = max(stop - start for start, stop in spans)
    starts = [start for start, _ in spans]
    if chunks is None or any(start + window > width for start in starts):
        return None
    ready = [
        max(starts[c] + window, width - starts[n_col - 1 - c]) for c in range(n_col)
    ]
    tail = head_cols % LANES
    fitting = [
        n
        for n in range(1, LANES // tail + 1 if tail else 2)
        if head_rows % (16 * n) == 0
    ]
    if not fitting or head_cols < LANES:
        return None
    return chunks, ready, window, head_rows // max(fitting)


def fused_body(n_row, n_col, pooled, text_embed, head_weight, logit_scale, logit_bias, partner):
    rows, width = pooled.shape
    factor = 1.0 / math.sqrt(rows * n_row * n_col)
    chunks, ready, window, tail_rows = plan_of(width, n_row, n_col)
    head_cols = width // n_col
    packed_rows = head_cols // LANES * (width // n_row)
    packed_rows += tail_rows if head_cols % LANES else 0
    bounds = [0, width // 8, width // 4, width // 2, width]
    spans = [aligned(bounds[q], bounds[q + 1]) for q in range(4)]
    masked_width = sum(stop - start for start, stop in spans)
    head_rows, head_cols = width // n_row, width // n_col
    vmem = pl.BlockSpec(memory_space=pltpu.VMEM)
    smem = pl.BlockSpec(memory_space=pltpu.SMEM)
    dma = pltpu.SemaphoreType.DMA
    return pl.pallas_call(
        functools.partial(
            kernel, n_row, n_col, factor, chunks, ready, window, tail_rows
        ),
        out_shape=(
            jax.ShapeDtypeStruct((rows, width), jnp.float32),
            jax.ShapeDtypeStruct((head_rows, head_cols), jnp.float32),
        ),
        in_specs=[vmem, vmem, pl.BlockSpec(memory_space=pl.ANY), smem, smem, vmem],
        out_specs=(vmem, vmem),
        scratch_shapes=[
            pltpu.VMEM(head_weight.shape, jnp.bfloat16),
            dma,
            pltpu.VMEM((rows, width), jnp.float32),
            pltpu.VMEM((rows, width), jnp.bfloat16),
            pltpu.VMEM((rows, width), jnp.bfloat16),
            pltpu.VMEM((rows, width), jnp.bfloat16),
            pltpu.VMEM((width, rows), jnp.bfloat16),
            pltpu.VMEM((head_rows, n_row * rows), jnp.bfloat16),
            pltpu.VMEM((rows, width), jnp.bfloat16),
            pltpu.VMEM((rows, masked_width), jnp.bfloat16),
            pltpu.VMEM((n_row * rows, width), jnp.bfloat16),
            pltpu.VMEM((head_rows, width), jnp.float32),
            pltpu.VMEM((n_col, packed_rows, LANES), jnp.bfloat16),
            pltpu.VMEM((n_col, packed_rows, LANES), jnp.bfloat16),
            dma((2,)),
            dma((2,)),
            dma((n_row,)),
            dma((n_row,)),
            dma((n_row + 1, chunks)),
            dma((n_row + 1, chunks)),
            dma((n_col,)),
            dma((n_col,)),
        ],
        compiler_params=pltpu.CompilerParams(collective_id=0, has_side_effects=True),
    )(pooled, text_embed, head_weight, logit_scale, logit_bias, partner)


def per_device(n_row, n_col):
    def run(pooled, text_embed, head_weight, logit_scale, logit_bias, partner):
        rows, width = pooled.shape
        fused = (
            n_row == 2**3
            and n_col > 1
            and rows == LANES
            and width % LANES == 0
            and width % (16 * n_row) == 0
            and width % n_col == 0
            and plan_of(width, n_row, n_col) is not None
        )
        args = (pooled, text_embed, head_weight, logit_scale, logit_bias, partner)
        return deliver(*fused_body(n_row, n_col, *args)) if fused else body(*args)

    return run


def solution(mesh):
    in_specs = (
        P(("row", "col"), None),
        P(("row", "col"), None),
        P(),
        P(),
        P(),
        P(("row", "col"), None),
    )
    out_specs = (P(("row", "col"), None), P("row", "col"))
    run = per_device(mesh.shape["row"], mesh.shape["col"])
    return jax.shard_map(run, mesh=mesh, in_specs=in_specs, out_specs=out_specs, check_vma=False)
```

```python
import functools
import math

import jax
import jax.numpy as jnp
from jax import lax
from jax.experimental import pallas as pl
from jax.experimental.pallas import tpu as pltpu
from jax.sharding import PartitionSpec as P

LANES = 128
MESH = pl.DeviceIdType.MESH


def shifted(value, axis, by):
    count = lax.axis_size(axis)
    return lax.ppermute(value, axis, [(i, (i + by) % count) for i in range(count)])


def segment_weights(image_part, text_part, positive, logit_scale, logit_bias, factor):
    model_width = image_part.shape[1]
    bounds = [0, model_width // 8, model_width // 4, model_width // 2, model_width]
    running = jnp.zeros((image_part.shape[0], text_part.shape[0]), jnp.float32)
    level_grads = []
    for prefix in range(4):
        low_end = bounds[prefix]
        high_end = bounds[prefix + 1]
        running = running + jnp.dot(
            image_part[:, low_end:high_end],
            text_part[:, low_end:high_end].T,
            preferred_element_type=jnp.float32,
        )
        logits = logit_scale[prefix] * running + logit_bias[prefix]
        level_grads.append((jax.nn.sigmoid(logits) - positive) * factor)
    weights = []
    carried = jnp.zeros_like(running)
    for prefix in range(3, -1, -1):
        carried = carried + logit_scale[prefix] * level_grads[prefix]
        weights.insert(0, carried.astype(jnp.bfloat16))
    return (weights, bounds)


def image_side(weights, bounds, text_part):
    pieces = []
    for prefix in range(4):
        pieces.append(
            jnp.dot(
                weights[prefix],
                text_part[:, bounds[prefix] : bounds[prefix + 1]],
                preferred_element_type=jnp.float32,
            )
        )
    return jnp.concatenate(pieces, 1)


def text_side(weights, bounds, image_part):
    pieces = []
    for prefix in range(4):
        pieces.append(
            jnp.dot(
                weights[prefix].T,
                image_part[:, bounds[prefix] : bounds[prefix + 1]],
                preferred_element_type=jnp.float32,
            )
        )
    return jnp.concatenate(pieces, 1)


def body(pooled, text_embed, head_weight, logit_scale, logit_bias, partner):
    block_rows = pooled.shape[0]
    factor = 1.0 / math.sqrt(block_rows * lax.axis_size("row") * lax.axis_size("col"))
    embedding = jnp.dot(pooled, head_weight, preferred_element_type=jnp.float32).astype(
        jnp.bfloat16
    )
    local_ids = jnp.arange(block_rows, dtype=jnp.int32)
    positive = (partner[0][:, None] == local_ids[None, :]).astype(jnp.float32)
    empty = jnp.zeros((block_rows, block_rows), jnp.float32)
    weights, bounds = segment_weights(
        embedding, text_embed, positive, logit_scale, logit_bias, factor
    )
    own_image = image_side(weights, bounds, text_embed)
    own_text = text_side(weights, bounds, embedding)
    behind = shifted(text_embed, "row", 1)
    weights, bounds = segment_weights(embedding, behind, empty, logit_scale, logit_bias, factor)
    cross_image = image_side(weights, bounds, behind)
    cross_text = text_side(weights, bounds, embedding)
    returned = shifted(cross_text.astype(jnp.bfloat16), "row", -1).astype(cross_text.dtype)
    text_grad = own_text + returned
    image_grad = own_image + cross_image
    column_block = lax.all_to_all(
        image_grad.astype(jnp.bfloat16), "col", split_axis=1, concat_axis=0, tiled=True
    ).astype(image_grad.dtype)
    group_rows = lax.all_gather(pooled, "col", axis=0, tiled=True)
    block_term = jnp.dot(
        group_rows.astype(jnp.float32).T, column_block, precision=lax.Precision.HIGHEST
    )
    head_grad = lax.psum_scatter(block_term, "row", scatter_dimension=0, tiled=True)
    return (text_grad, head_grad)


def dot_nt(left, right):
    return lax.dot_general(
        left, right, (((1,), (1,)), ((), ())), preferred_element_type=jnp.float32
    )


def dot_nn(left, right):
    return jnp.dot(left, right, preferred_element_type=jnp.float32)


def aligned(low_end, high_end):
    return low_end // LANES * LANES, -(-high_end // LANES) * LANES


def weights_of(score_of, positive, scale_ref, bias_ref, factor):
    running = None
    level_grads = []
    for prefix in range(4):
        part = score_of(prefix)
        running = part if running is None else running + part
        gate = jax.nn.sigmoid(scale_ref[prefix] * running + bias_ref[prefix])
        if positive is not None:
            gate = gate - positive
        level_grads.append(gate * factor)
    weights = [None] * 4
    carried = None
    for prefix in range(3, -1, -1):
        term = scale_ref[prefix] * level_grads[prefix]
        carried = term if carried is None else carried + term
        weights[prefix] = carried.astype(jnp.bfloat16)
    return weights


def by_tile(piece_of, bounds, store):
    pieces = []
    for q in range(4):
        start, stop = aligned(bounds[q], bounds[q + 1])
        pieces.append((start, stop, piece_of(q, start, stop)))
    for tile in range(bounds[4] // LANES):
        base = tile * LANES
        value = None
        for q in range(4):
            start, stop, piece = pieces[q]
            if start <= base < stop:
                here = piece[:, base - start : base - start + LANES]
                if value is None:
                    value = here
                else:
                    lane = lax.broadcasted_iota(jnp.int32, here.shape, 1)
                    value = jnp.where(lane < bounds[q] - base, value, here)
        store(base, value)


def kernel(
    n_row,
    n_col,
    factor,
    chunks,
    ready,
    window,
    tail_rows,
    pooled_ref,
    text_ref,
    weight_hbm,
    scale_ref,
    bias_ref,
    partner_ref,
    text_grad_ref,
    head_grad_ref,
    weight_ref,
    weight_sem,
    image_own,
    cross_text,
    text_back,
    text_behind,
    pooled_t,
    pooled_cols,
    embed,
    masked,
    image,
    total,
    sent,
    landed,
    near_send,
    near_recv,
    pool_send,
    pool_recv,
    image_send,
    image_recv,
    out_send,
    out_recv,
):
    rows, width = pooled_ref.shape
    chips = n_row // 2
    head_rows = width // n_row
    head_cols = width // n_col
    bounds = [0, width // 8, width // 4, width // 2, width]
    row = lax.axis_index("row")
    col = lax.axis_index("col")
    chip = row // 2
    core = row % 2

    side = chip % 2
    level = chip // 2

    def peer(k, e):
        there = chip + (k % 2) * (1 - 2 * side) + (k // 2) * (2 - 4 * level)
        return there * 2 + (core if e == 0 else 1 - core)

    weight_copy = pltpu.make_async_copy(weight_hbm, weight_ref, weight_sem)
    weight_copy.start()

    barrier = pltpu.get_barrier_semaphore()
    for d in range(1, n_row):
        pl.semaphore_signal(
            barrier, inc=1, device_id=((row + d) % n_row, col), device_id_type=MESH
        )
    for d in range(1, n_col):
        pl.semaphore_signal(
            barrier, inc=1, device_id=(row, (col + d) % n_col), device_id_type=MESH
        )

    def remote(src, dst, send, recv, device):
        return pltpu.make_async_remote_copy(
            src_ref=src,
            dst_ref=dst,
            send_sem=send,
            recv_sem=recv,
            device_id=device,
            device_id_type=MESH,
        )

    behind_copy = remote(
        text_ref, text_behind, near_send.at[0], near_recv.at[0], ((row + 1) % n_row, col)
    )
    back_copy = remote(
        cross_text,
        text_back,
        near_send.at[1],
        near_recv.at[1],
        ((row + n_row - 1) % n_row, col),
    )
    pl.semaphore_wait(barrier, n_row + n_col - 2)
    behind_copy.start()

    for tile in range(width // LANES):
        lanes = pl.ds(tile * LANES, LANES)
        pooled_t[lanes, :] = pooled_ref[:, lanes].T
    pool_copies = []
    for k in range(chips):
        for e in range(2):
            slot = 2 * k + e
            if slot == 0:
                continue
            target = peer(k, e)
            copy = remote(
                pooled_t.at[pl.ds(pl.multiple_of(target * head_rows, 16), head_rows), :],
                pooled_cols.at[:, pl.ds(slot * rows, rows)],
                pool_send.at[slot],
                pool_recv.at[slot],
                (target, col),
            )
            pool_copies.append(copy)
    pooled_cols[:, pl.ds(0, rows)] = pooled_t[
        pl.ds(pl.multiple_of(row * head_rows, 16), head_rows), :
    ]

    def fill_embed(source):
        at = 0
        for q in range(4):
            start, stop = aligned(bounds[q], bounds[q + 1])
            at += stop - start
        step = 3 * LANES if width % (3 * LANES) == 0 else LANES
        for base in range(0, width, step):
            part = dot_nn(source[...], weight_ref[:, pl.ds(base, step)])
            embed[:, pl.ds(base, step)] = part.astype(jnp.bfloat16)
        at = 0
        for q in range(4):
            start, stop = aligned(bounds[q], bounds[q + 1])
            part = embed[:, pl.ds(start, stop - start)].astype(jnp.float32)
            lane = lax.broadcasted_iota(jnp.int32, part.shape, 1) + start
            keep = (lane >= bounds[q]) & (lane < bounds[q + 1])
            masked[:, pl.ds(at, stop - start)] = jnp.where(keep, part, 0.0).astype(
                jnp.bfloat16
            )
            at += stop - start

    def masked_part(q):
        at = 0
        for before in range(q):
            start, stop = aligned(bounds[before], bounds[before + 1])
            at += stop - start
        start, stop = aligned(bounds[q], bounds[q + 1])
        return masked[:, pl.ds(at, stop - start)]

    def text_part(ref, q):
        start, stop = aligned(bounds[q], bounds[q + 1])
        return ref[:, pl.ds(start, stop - start)]

    for copy in pool_copies:
        copy.start()
    weight_copy.wait()
    fill_embed(pooled_ref)
    text_id = lax.broadcasted_iota(jnp.int32, (rows, rows), 0)
    positive = (text_id == partner_ref[...]).astype(jnp.float32).T
    own = weights_of(
        lambda q: dot_nt(masked_part(q), text_part(text_ref, q)),
        positive,
        scale_ref,
        bias_ref,
        factor,
    )

    def own_image_piece(q, start, stop):
        return dot_nn(own[q], text_ref[:, pl.ds(start, stop - start)])

    def keep_image(base, value):
        image_own[:, pl.ds(base, LANES)] = value

    by_tile(own_image_piece, bounds, keep_image)

    def own_text_piece(q, start, stop):
        return dot_nn(own[q].T, embed[:, pl.ds(start, stop - start)])

    def store_text(base, value):
        text_grad_ref[:, pl.ds(base, LANES)] = value

    by_tile(own_text_piece, bounds, store_text)

    behind_copy.wait_recv()
    cross = weights_of(
        lambda q: dot_nt(masked_part(q), text_part(text_behind, q)),
        None,
        scale_ref,
        bias_ref,
        factor,
    )

    def image_piece(q, start, stop):
        lanes = pl.ds(start, stop - start)
        return dot_nn(cross[q], text_behind[:, lanes])

    def store_image(base, value):
        lanes = pl.ds(base, LANES)
        image[pl.ds(0, rows), lanes] = (image_own[:, lanes] + value).astype(jnp.bfloat16)

    by_tile(image_piece, bounds, store_image)

    chunk = width // chunks
    half = rows // 2
    flip = (2 * col >= n_col).astype(jnp.int32)

    def mirrored(index, count):
        return flip * index + (1 - flip) * (count - 1 - index)

    def piece_of(slot, i, first=0, count=rows):
        lanes = pl.ds(pl.multiple_of(mirrored(i, chunks) * chunk, LANES), chunk)
        return image.at[pl.ds(slot * rows + first, count), lanes]

    image_copies = {}

    def send_image(name, src_slot, dst_slot, i, target, first=0, count=rows):
        image_copies[name, i] = remote(
            piece_of(src_slot, i, first, count),
            piece_of(dst_slot, i, first, count),
            image_send.at[name, i],
            image_recv.at[name, i],
            (target, col),
        )
        image_copies[name, i].start()

    def send_own(i):
        send_image(2, 0, 2, i, peer(1, 0))
        send_image(4, 0, 4, i, peer(2, 0))
        send_image(1, 0, 1, i, peer(0, 1))

    def pass_direct(i):
        image_copies[2, i].wait_recv()
        send_image(6, 2, 6, i, peer(2, 0), 0, half)
        send_image(3, 2, 3, i, peer(0, 1))
        image_copies[4, i].wait_recv()
        send_image(8, 4, 6, i, peer(1, 0), half, half)
        send_image(5, 4, 5, i, peer(0, 1))

    def pass_corner(i):
        image_copies[6, i].wait_recv()
        image_copies[8, i].wait_recv()
        send_image(7, 6, 7, i, peer(0, 1))

    for i in range(chunks - 1):
        send_own(i)

    def cross_text_piece(q, start, stop):
        return dot_nn(cross[q].T, embed[:, pl.ds(start, stop - start)])

    def store_cross(base, value):
        cross_text[:, pl.ds(base, LANES)] = value.astype(jnp.bfloat16)

    by_tile(cross_text_piece, bounds, store_cross)

    pass_direct(0)
    send_own(chunks - 1)
    pass_corner(0)
    for i in range(1, chunks):
        pass_direct(i)
    for i in range(1, chunks - 1):
        pass_corner(i)
    back_copy.start()

    main = head_cols // LANES * LANES
    tail = head_cols - main
    groups = head_rows // tail_rows

    def lanes_of(block):
        first = block * head_cols // LANES * LANES
        offset = block * head_cols - first
        part = total[:, pl.ds(pl.multiple_of(first, LANES), window)]
        return pltpu.roll(part, (window - offset) % window, 1)

    def packed(block):
        part = lanes_of(block)
        parts = [part[:, base : base + LANES] for base in range(0, main, LANES)]
        if tail:
            last = part[:, main : main + LANES]
            lane = lax.broadcasted_iota(jnp.int32, last.shape, 1)
            last = jnp.where(lane < tail, last, 0.0)
            joined = last[:tail_rows]
            for j in range(1, groups):
                here = last[j * tail_rows : (j + 1) * tail_rows]
                joined = joined + pltpu.roll(here, j * tail, 1)
            parts.append(joined)
        return parts

    def out_copy(block):
        return remote(
            sent.at[block],
            landed.at[col],
            out_send.at[block],
            out_recv.at[col],
            (row, block),
        )

    def in_copy(block):
        return remote(
            sent.at[block],
            landed.at[block],
            out_send.at[block],
            out_recv.at[block],
            (row, block),
        )

    for copy in pool_copies:
        copy.wait_recv()
    done = 0
    for i in range(chunks):
        if i == chunks - 1:
            pass_corner(i)
        image_copies[1, i].wait_recv()
        for slot in (3, 5, 7):
            image_copies[slot, i].wait_recv()
        lanes = pl.ds(pl.multiple_of(mirrored(i, chunks) * chunk, LANES), chunk)
        total[:, lanes] = dot_nn(pooled_cols[...], image[:, lanes])
        while done < n_col and ready[done] <= (i + 1) * chunk:
            block = mirrored(done, n_col)

            @pl.when(block != col)
            def _():
                at = 0
                for part in packed(block):
                    count = part.shape[0]
                    sent[block, pl.ds(at, count), :] = part.astype(jnp.bfloat16)
                    at += count
                out_copy(block).start()

            done += 1

    back_copy.wait_recv()
    text_grad_ref[...] = text_grad_ref[...] + text_back[...].astype(jnp.float32)

    results = packed(col)
    for d in range(n_col - 1, 0, -1):
        block = (col + d) % n_col
        in_copy(block).wait_recv()
        at = 0
        for n, part in enumerate(results):
            count = part.shape[0]
            got = landed[block, pl.ds(at, count), :]
            results[n] = part + got.astype(jnp.float32)
            at += count
    for n in range(main // LANES):
        head_grad_ref[:, pl.ds(n * LANES, LANES)] = results[n]
    if tail:
        for j in range(groups):
            here = results[-1]
            if j > 0:
                here = pltpu.roll(here, LANES - j * tail, 1)
            head_grad_ref[pl.ds(j * tail_rows, tail_rows), pl.ds(main, tail)] = here[:, :tail]

    behind_copy.wait_send()
    back_copy.wait_send()
    for copy in pool_copies:
        copy.wait_send()
    for name in sorted(image_copies):
        image_copies[name].wait_send()
    for d in range(1, n_col):
        in_copy((col + d) % n_col).wait_send()


def deliver(text_grad, head_grad):
    parts = 4
    step = text_grad.shape[0] // parts

    def move(text_from, head_from, text_to, head_to, text_held, head_held, sems, head_sems):
        def rows_of(ref, n):
            return ref.at[pl.ds(n * step, step), :]

        loads = [
            pltpu.make_async_copy(rows_of(text_from, n), rows_of(text_held, n), sems.at[0, n])
            for n in range(parts)
        ]
        head_load = pltpu.make_async_copy(head_from, head_held, head_sems.at[0])
        for load in loads:
            load.start()
        head_load.start()
        stores = []
        for n in range(parts):
            loads[n].wait()
            stores.append(
                pltpu.make_async_copy(rows_of(text_held, n), rows_of(text_to, n), sems.at[1, n])
            )
            stores[n].start()
        head_load.wait()
        head_store = pltpu.make_async_copy(head_held, head_to, head_sems.at[1])
        head_store.start()
        for store in stores:
            store.wait()
        head_store.wait()

    anywhere = pl.BlockSpec(memory_space=pl.ANY)
    return pl.pallas_call(
        move,
        out_shape=(
            jax.ShapeDtypeStruct(text_grad.shape, text_grad.dtype),
            jax.ShapeDtypeStruct(head_grad.shape, head_grad.dtype),
        ),
        in_specs=[anywhere, anywhere],
        out_specs=(anywhere, anywhere),
        scratch_shapes=[
            pltpu.VMEM(text_grad.shape, text_grad.dtype),
            pltpu.VMEM(head_grad.shape, head_grad.dtype),
            pltpu.SemaphoreType.DMA((2, parts)),
            pltpu.SemaphoreType.DMA((2,)),
        ],
    )(text_grad, head_grad)


def plan_of(width, n_row, n_col):
    head_rows, head_cols = width // n_row, width // n_col
    chunks = next((n for n in (3, 2, 1) if width % (n * LANES) == 0), None)
    spans = [aligned(c * head_cols, (c + 1) * head_cols) for c in range(n_col)]
    window = max(stop - start for start, stop in spans)
    starts = [start for start, _ in spans]
    if chunks is None or any(start + window > width for start in starts):
        return None
    ready = [
        max(starts[c] + window, width - starts[n_col - 1 - c]) for c in range(n_col)
    ]
    tail = head_cols % LANES
    fitting = [
        n
        for n in range(1, LANES // tail + 1 if tail else 2)
        if head_rows % (16 * n) == 0
    ]
    if not fitting or head_cols < LANES:
        return None
    return chunks, ready, window, head_rows // max(fitting)


def fused_body(n_row, n_col, pooled, text_embed, head_weight, logit_scale, logit_bias, partner):
    rows, width = pooled.shape
    factor = 1.0 / math.sqrt(rows * n_row * n_col)
    chunks, ready, window, tail_rows = plan_of(width, n_row, n_col)
    head_cols = width // n_col
    packed_rows = head_cols // LANES * (width // n_row)
    packed_rows += tail_rows if head_cols % LANES else 0
    bounds = [0, width // 8, width // 4, width // 2, width]
    spans = [aligned(bounds[q], bounds[q + 1]) for q in range(4)]
    masked_width = sum(stop - start for start, stop in spans)
    head_rows, head_cols = width // n_row, width // n_col
    vmem = pl.BlockSpec(memory_space=pltpu.VMEM)
    smem = pl.BlockSpec(memory_space=pltpu.SMEM)
    dma = pltpu.SemaphoreType.DMA
    return pl.pallas_call(
        functools.partial(
            kernel, n_row, n_col, factor, chunks, ready, window, tail_rows
        ),
        out_shape=(
            jax.ShapeDtypeStruct((rows, width), jnp.float32),
            jax.ShapeDtypeStruct((head_rows, head_cols), jnp.float32),
        ),
        in_specs=[vmem, vmem, pl.BlockSpec(memory_space=pl.ANY), smem, smem, vmem],
        out_specs=(vmem, vmem),
        scratch_shapes=[
            pltpu.VMEM(head_weight.shape, jnp.bfloat16),
            dma,
            pltpu.VMEM((rows, width), jnp.float32),
            pltpu.VMEM((rows, width), jnp.bfloat16),
            pltpu.VMEM((rows, width), jnp.bfloat16),
            pltpu.VMEM((rows, width), jnp.bfloat16),
            pltpu.VMEM((width, rows), jnp.bfloat16),
            pltpu.VMEM((head_rows, n_row * rows), jnp.bfloat16),
            pltpu.VMEM((rows, width), jnp.bfloat16),
            pltpu.VMEM((rows, masked_width), jnp.bfloat16),
            pltpu.VMEM((n_row * rows, width), jnp.bfloat16),
            pltpu.VMEM((head_rows, width), jnp.float32),
            pltpu.VMEM((n_col, packed_rows, LANES), jnp.bfloat16),
            pltpu.VMEM((n_col, packed_rows, LANES), jnp.bfloat16),
            dma((2,)),
            dma((2,)),
            dma((n_row,)),
            dma((n_row,)),
            dma((n_row + 1, chunks)),
            dma((n_row + 1, chunks)),
            dma((n_col,)),
            dma((n_col,)),
        ],
        compiler_params=pltpu.CompilerParams(collective_id=0, has_side_effects=True),
    )(pooled, text_embed, head_weight, logit_scale, logit_bias, partner)


def per_device(n_row, n_col):
    def run(pooled, text_embed, head_weight, logit_scale, logit_bias, partner):
        rows, width = pooled.shape
        fused = (
            n_row == 2**3
            and n_col > 1
            and rows == LANES
            and width % LANES == 0
            and width % (16 * n_row) == 0
            and width % n_col == 0
            and plan_of(width, n_row, n_col) is not None
        )
        args = (pooled, text_embed, head_weight, logit_scale, logit_bias, partner)
        return deliver(*fused_body(n_row, n_col, *args)) if fused else body(*args)

    return run


def solution(mesh):
    in_specs = (
        P(("row", "col"), None),
        P(("row", "col"), None),
        P(),
        P(),
        P(),
        P(("row", "col"), None),
    )
    out_specs = (P(("row", "col"), None), P("row", "col"))
    run = per_device(mesh.shape["row"], mesh.shape["col"])
    return jax.shard_map(run, mesh=mesh, in_specs=in_specs, out_specs=out_specs, check_vma=False)
```
